512 devices in a mesh: pb: 128 (over y, z, core), slab: 4 (over x).
Axes of the slice: x: 4, y: 4, z: 16, core: 2. Of those that a mesh axis runs over, the one named last changes fastest.
Arguments:
- query_feats: bfloat16 [128, 128, 9, 256], P('pb', 'slab'), may hold values from -1.5 to 1.5
- frame_store: bfloat16 [512, 128, 9, 256], P(None, 'pb'), may hold values from -1.5 to 1.5
- candidates: int32 [128, 4], replicated, may hold values from 0 to 511
- query_length: int32 [128], P('pb'), may hold values from 16 to 128, as said below
- clip_length: int32 [512], replicated, may hold values from 16 to 128, as said below
- kernel_one: float32 [3, 3, 1, 32], replicated, may hold values from -2 to 2
- bias_one: float32 [32], replicated, may hold values from -0.2 to 0.2
- kernel_two: float32 [3, 3, 32, 64], replicated, may hold values from -0.375 to 0.375
- bias_two: float32 [64], replicated, may hold values from -0.2 to 0.2
- kernel_three: float32 [3, 3, 64, 128], replicated, may hold values from -0.25 to 0.25
- bias_three: float32 [128], replicated, may hold values from -0.2 to 0.2
- kernel_four: float32 [1, 1, 128, 1], replicated, may hold values from -0.5 to 0.5
- bias_four: float32 [1], replicated, may hold values from -1.75 to 1.75
Outputs:
- scores: float32 [128, 4], P('pb')
The draws below stay inside these ranges and needn't reach their ends.
Inputs may be any that keep to these rules, and one draw needn't show every extreme that they name: `query_length`: some query has exactly 128 valid frames and some exactly 16. `clip_length`: some candidate clip has exactly 128 valid frames and some exactly 16.
All inputs are finite; a program needn't handle non-finite values.
Results may differ from the reference program's by a relative error of at most 0.0003.
Values may be sent and summed in bfloat16 or wider, within the bound.
A program may use at most 128 MiB of HBM per device.

```python
import jax
import jax.numpy as jnp
from jax import lax

F = 128
R = 9
C = 256
K1 = 32
K2 = 64
K3 = 128
P_SIZE = 4
QUERIES = 128
CLIPS = 512


def draw_bounded(key, amount, lowest, highest):
    keys = jax.random.split(key, 3)
    values = jax.random.randint(keys[0], (amount,), lowest, highest + 1)
    place_high = jax.random.randint(keys[1], (), 0, amount)
    place_low = (place_high + jax.random.randint(keys[2], (), 1, amount)) % amount
    values = values.at[place_high].set(highest)
    values = values.at[place_low].set(lowest)
    return values.astype(jnp.int32)


def draw_query_length(key, part):
    return draw_bounded(jax.random.fold_in(key, 11), QUERIES, 16, F)


def draw_clip_length(key, part):
    return draw_bounded(jax.random.fold_in(key, 23), CLIPS, 16, F)


def place_ends(values, key, low, largest):
    longest = values.shape.index(max(values.shape))
    spots = []
    for shift in (0, 1):
        where = [jax.random.randint(jax.random.fold_in(key, axis), (), 0, length) for axis, length in enumerate(values.shape)]
        where[longest] = (where[longest] + shift) % values.shape[longest]
        spots.append(tuple(where))
    return values.at[spots[0]].set(low).at[spots[1]].set(largest)


def levels(stream_key, extent, cuts, least, largest):
    level = 1.0
    for position, parts in cuts:
        draws = jax.random.uniform(jax.random.fold_in(jax.random.fold_in(stream_key, 6), position), (parts,), jnp.float32, least / len(cuts), largest / len(cuts))
        level = level * jnp.repeat(jnp.exp(draws), extent[position] // parts).reshape((-1,) + (1,) * (len(extent) - 1 - position))
    return level


def noise(rng, shape, deviation, reach, cuts=(), held_as=jnp.bfloat16):
    entries = deviation * jax.random.normal(rng, shape, jnp.float32)
    if cuts:
        entries = entries * levels(rng, shape, cuts, -0.22, 0.18)
    return jnp.clip(entries, -reach, reach).astype(held_as)


def setup_inputs(seed: int = 0) -> dict:
    key_of = jax.random.split(jax.random.key(seed), 14)
    query_feats = noise(key_of[0], (QUERIES, F, R, C), (C ** 0.5) ** -0.5, 1.5, ((0, 128), (1, 4)))
    frame_store = noise(key_of[1], (CLIPS, F, R, C), (C ** 0.5) ** -0.5, 1.5, ((1, 128),))
    candidates = place_ends(jax.random.randint(key_of[2], (QUERIES, P_SIZE), 0, CLIPS), jax.random.fold_in(key_of[2], 1), 0, CLIPS - 1).astype(jnp.int32)
    query_length = draw_query_length(jax.random.fold_in(key_of[13], 71), 0)
    clip_length = draw_clip_length(jax.random.fold_in(key_of[13], 71), 0)
    kernel_one = noise(key_of[5], (3, 3, 1, K1), 9 ** -0.5, 2.0, (), jnp.float32)
    bias_one = jnp.clip(jax.random.uniform(key_of[6], (K1,), jnp.float32, -0.2, 0.2), -0.2, 0.2)
    kernel_two = noise(key_of[7], (3, 3, K1, K2), (9 * K1) ** -0.5, 0.375, (), jnp.float32)
    bias_two = jnp.clip(jax.random.uniform(key_of[8], (K2,), jnp.float32, -0.2, 0.2), -0.2, 0.2)
    kernel_three = noise(key_of[9], (3, 3, K2, K3), (9 * K2) ** -0.5, 0.25, (), jnp.float32)
    bias_three = jnp.clip(jax.random.uniform(key_of[10], (K3,), jnp.float32, -0.2, 0.2), -0.2, 0.2)
    kernel_four = noise(key_of[11], (1, 1, K3, 1), K3 ** -0.5, 0.5, (), jnp.float32)
    bias_four = noise(key_of[12], (1,), 0.3, 1.75, (), jnp.float32)
    return {"query_feats": query_feats, "frame_store": frame_store, "candidates": candidates, "query_length": query_length, "clip_length": clip_length, "kernel_one": kernel_one, "bias_one": bias_one, "kernel_two": kernel_two, "bias_two": bias_two, "kernel_three": kernel_three, "bias_three": bias_three, "kernel_four": kernel_four, "bias_four": bias_four}


def region_map(features, clip):
    feature_width = features.shape[-1]
    gram = lax.dot_general(features.reshape(-1, feature_width), clip.reshape(-1, feature_width), (((1,), (1,)), ((), ())), preferred_element_type=jnp.float32)
    gram = gram.reshape(features.shape[0], features.shape[1], clip.shape[0], clip.shape[1])
    return jnp.mean(jnp.max(gram, axis=3), axis=1)


def conv_same(field, kernel, bias):
    result = lax.conv_general_dilated(field, kernel, (1, 1), ((1, 1), (1, 1)), dimension_numbers=("NHWC", "HWIO", "NHWC"), precision=lax.Precision.HIGHEST)
    return result + bias


def point_conv(field, kernel, bias):
    result = jnp.einsum("nhwk,ko->nhwo", field, kernel[0, 0], precision=lax.Precision.HIGHEST)
    return result + bias


def pool_pairs(field):
    shape_now = field.shape
    blocks = field.reshape(shape_now[0], shape_now[1] // 2, 2, shape_now[2] // 2, 2, shape_now[3])
    return jnp.max(blocks, axis=(2, 4))


def reference(query_feats, frame_store, candidates, query_length, clip_length, kernel_one, bias_one, kernel_two, bias_two, kernel_three, bias_three, kernel_four, bias_four):
    positions = jnp.arange(F, dtype=jnp.int32)
    pooled = jnp.arange(F // 4, dtype=jnp.int32)

    def per_query(packed):
        features, length_now, clip_ids = packed
        clips = frame_store[clip_ids]

        def single_clip(clip):
            return region_map(features, clip)

        maps = lax.map(single_clip, clips)
        pair_length = clip_length[clip_ids]
        row_valid = positions < length_now
        col_valid = positions[None, :] < pair_length[:, None]
        masked = jnp.where(row_valid[None, :, None] & col_valid[:, None, :], maps, 0.0)
        layer_one = pool_pairs(jax.nn.relu(conv_same(masked[..., None], kernel_one, bias_one)))
        layer_two = pool_pairs(jax.nn.relu(conv_same(layer_one, kernel_two, bias_two)))
        layer_three = jax.nn.relu(conv_same(layer_two, kernel_three, bias_three))
        final_maps = jnp.clip(point_conv(layer_three, kernel_four, bias_four)[..., 0], -1.0, 1.0)
        col_keep = 4 * pooled[None, :] < pair_length[:, None]
        row_keep = 4 * pooled < length_now
        row_best = jnp.max(jnp.where(col_keep[:, None, :], final_maps, -2.0), axis=2)
        row_total = jnp.sum(jnp.where(row_keep[None, :], row_best, 0.0), axis=1)
        row_number = ((length_now + 3) // 4).astype(jnp.float32)
        return row_total / row_number

    return lax.map(per_query, (query_feats, query_length, candidates))
```

```python
import functools

import jax
import jax.numpy as jnp
from jax import lax
from jax.experimental import pallas as pl
from jax.experimental.pallas import tpu as pltpu
from jax.sharding import PartitionSpec as P

NY, NZ, NC, NX = 4, 16, 2, 4
NSLOT = NY * NC
NCHUNK = 3
SPER = 3
MESH = pl.DeviceIdType.MESH
BF = jnp.bfloat16
F32 = jnp.float32
Z_ORDER = (8, 7, 9, 6, 10, 5, 11, 4, 12, 3, 13, 2, 14, 1, 15)


def iota(shape, dim):
    return lax.broadcasted_iota(jnp.int32, shape, dim)


def dot(a, b):
    return lax.dot_general(a, b, (((1,), (0,)), ((), ())), preferred_element_type=F32)


def dot_t(a, b):
    return lax.dot_general(a, b, (((1,), (1,)), ((), ())), preferred_element_type=F32)


def hot(mask):
    return jnp.where(mask, 1.0, 0.0).astype(BF)


def halves(x):
    hi = x.astype(BF)
    lo = (x - hi.astype(F32)).astype(BF)
    return hi, lo


def prepare(k1, b1, k2, b2, k3, b3, k4, sq, w1, w2, w3, b2c, k4c, p1f, p1b, p3h, p3l):
    sq[...] = jnp.zeros_like(sq)
    for tap in range(9):
        sq[tap : tap + 1, 0:32] = k1[tap]
    sq[9:10, 0:32] = b1[...]
    hi, lo = halves(jnp.transpose(sq[...])[0:32])
    t = iota((128, 256), 0)
    k = iota((128, 256), 1)
    ti = jnp.where(t >= 3, 1, 0) + jnp.where(t >= 6, 1, 0)
    tj = t - 3 * ti
    for phase in range(16):
        row = 2 * (phase >> 3) + ((phase >> 1) & 1)
        col = 2 * ((phase >> 2) & 1) + (phase & 1)
        at = jnp.where(t == 9, 36, (row + ti) * 6 + col + tj)
        at = jnp.where(t > 9, -1000, at)
        both = hot((k == at) | (k == at + 48))
        last = hot(k == at + 96)
        w1[phase * 32 : phase * 32 + 32, :] = (dot(hi, both) + dot(lo, last)).astype(BF)
    w2[...] = jnp.zeros_like(w2)
    for ti in range(3):
        sq[...] = jnp.zeros_like(sq)
        sq[0:96, 0:64] = k2[ti * 96 : ti * 96 + 96, :]
        block = jnp.transpose(sq[...])[0:64]
        for a in range(2):
            for b in range(2):
                hi, lo = halves(block if b == 0 else pltpu.roll(block, 32, 1))
                lanes = slice((a + ti) * 128, (a + ti) * 128 + 128)
                row = (a * 2 + b) * 64
                w2[row : row + 64, lanes] = hi
                w2[256 + row : 256 + row + 64, lanes] = lo
    sq[...] = jnp.zeros_like(sq)
    sq[:, 0:64] = jnp.broadcast_to(b2[...], (128, 64))
    b2c[...] = jnp.transpose(sq[...])[0:64]
    for part in range(5):
        if part < 4:
            block = k3[part * 128 : part * 128 + 128, :]
        else:
            sq[...] = jnp.zeros_like(sq)
            sq[0:64, :] = k3[512:576, :]
            sq[64:65, :] = b3[...]
            block = sq[...]
        hi, lo = halves(jnp.transpose(block))
        w3[0:128, part * 128 : part * 128 + 128] = hi
        w3[128:256, part * 128 : part * 128 + 128] = lo
    k4c[...] = jnp.transpose(jnp.broadcast_to(k4[...], (128, 128)))
    p1b[144:256, :] = jnp.zeros((112, 1024), BF)
    ones = jnp.where(iota((16, 128), 0) == 4, 1.0, 0.0)
    for u in range(8):
        p1f[u * 48 + 32 : u * 48 + 48, :] = ones
    p3h[576:640, :] = hot(iota((64, 1024), 0) == 0)
    p3l[576:640, :] = jnp.zeros((64, 1024), BF)


def gram_chunk(chunk, qbuf, x, best):
    blocks = []
    for s in range(SPER):
        for e in range(2):
            blocks.append(x[chunk, :, s, e].reshape(64, 256))
    right = jnp.concatenate(blocks, axis=0)
    for r in range(9):
        g = dot_t(qbuf[:, r].reshape(128, 256), right)
        m = jnp.maximum(jnp.maximum(g[:, 0:128], g[:, 128:256]), g[:, 256:384])
        best[r] = m if chunk == 0 else jnp.maximum(best[r], m)


def refine(best, qlen, clen, b4, w1, w2, w3, b2c, k4c, p1f, p1b, p2h, p2l, p3h, p3l):
    lane = iota((8, 128), 1)
    sub = iota((8, 128), 0)
    grp = lane >> 5
    col = lane & 31
    total = best[0]
    for r in range(1, 9):
        total = total + best[r]
    total = total * (1.0 / 9.0)
    keep_col = (4 * col + grp) < clen
    sim = []
    for g in range(4):
        line = []
        for sg in range(4):
            at = (g * 4 + sg) * 8
            keep = keep_col & ((32 * g + 4 * sub + sg) < qlen)
            line.append(jnp.where(keep, total[at : at + 8], 0.0))
        sim.append(line)

    def up(x, nrow):
        y = pltpu.roll(x, 1, 0)
        z = jnp.where(grp == 0, 0.0, pltpu.roll(y, 32, 1))
        return jnp.where(sub == 0, z, y)

    def down(x, nrow):
        y = pltpu.roll(x, 7, 0)
        z = jnp.where(grp == 3, 0.0, pltpu.roll(y, 96, 1))
        return jnp.where(sub == 7, z, y)

    base = {}
    for sg in range(4):
        for rho in range(4):
            out = None
            for g in range(4):
                shift = ((g - rho) * 32) % 128
                piece = sim[g][sg] if shift == 0 else pltpu.roll(sim[g][sg], shift, 1)
                out = piece if out is None else jnp.where(grp == g, piece, out)
            base[sg, rho] = out
    rows = {}
    for rho in range(4):
        for sg in range(4):
            rows[sg, rho] = base[sg, rho]
        rows[-1, rho] = up(base[3, rho], 8)
        rows[4, rho] = down(base[0, rho], 8)
    for d in range(-1, 5):
        for e in range(-1, 5):
            if e == -1:
                v = jnp.where(col == 0, 0.0, pltpu.roll(rows[d, 3], 1, 1))
            elif e == 4:
                v = jnp.where(col == 31, 0.0, pltpu.roll(rows[d, 0], 127, 1))
            else:
                v = rows[d, e]
            p1f[pl.ds((d + 1) * 6 + e + 1, 8, stride=48), :] = v
    for u in range(8):
        hi, lo = halves(p1f[u * 48 : u * 48 + 48, :])
        lanes = slice(u * 128, u * 128 + 128)
        p1b[0:48, lanes] = hi
        p1b[48:96, lanes] = lo
        p1b[96:144, lanes] = hi

    def tall(x, n):
        return jnp.broadcast_to(x[0:1], (n, 128))

    grp32, col32 = tall(grp, 32), tall(col, 32)
    grp64, col64 = tall(grp, 64), tall(col, 64)

    def put(high, low, at, n, u, value):
        hi, lo = halves(value)
        high[at : at + n, u * 128 : u * 128 + 128] = hi
        low[at : at + n, u * 128 : u * 128 + 128] = lo
        return hi, lo

    def put_above(high, low, at, n, u, value, pair, groups):
        if u < 7:
            high[at : at + n, u * 128 + 128 : u * 128 + 256] = pair[0]
            low[at : at + n, u * 128 + 128 : u * 128 + 256] = pair[1]
        else:
            put(high, low, at, n, 0, jnp.where(groups == 0, 0.0, pltpu.roll(value, 32, 1)))

    def put_below(high, low, at, n, u, value, pair, groups):
        if u > 0:
            high[at : at + n, u * 128 - 128 : u * 128] = pair[0]
            low[at : at + n, u * 128 - 128 : u * 128] = pair[1]
        else:
            put(high, low, at, n, 7, jnp.where(groups == 3, 0.0, pltpu.roll(value, 96, 1)))

    for tile in range(4):
        o1 = dot(w1[...], p1b[:, tile * 256 : tile * 256 + 256])
        for ab in range(4):
            a, b = ab >> 1, ab & 1
            part = o1[ab * 128 : ab * 128 + 128]
            m = jnp.maximum(
                jnp.maximum(part[0:32], part[32:64]), jnp.maximum(part[64:96], part[96:128])
            )
            m = jnp.maximum(m, 0.0)
            for half in range(2):
                u = tile * 2 + half
                v = m[:, half * 128 : half * 128 + 128]
                if b == 1:
                    moved = jnp.where(col32 == 0, 0.0, pltpu.roll(v, 1, 1))
                    variants = ((2, v), (0, moved))
                else:
                    moved = jnp.where(col32 == 31, 0.0, pltpu.roll(v, 127, 1))
                    variants = ((1, v), (3, moved))
                for e, w in variants:
                    if a == 0:
                        pair = put(p2h, p2l, (4 + e) * 32, 32, u, w)
                        put_below(p2h, p2l, (12 + e) * 32, 32, u, w, pair, grp32)
                    else:
                        pair = put(p2h, p2l, (8 + e) * 32, 32, u, w)
                        put_above(p2h, p2l, e * 32, 32, u, w, pair, grp32)
    for tile in range(4):
        lanes = slice(tile * 256, tile * 256 + 256)
        first = dot(w2[...], p2h[:, lanes])
        o2 = first[0:256] + (first[256:512] + dot(w2[0:256, :], p2l[:, lanes]))
        m = jnp.maximum(
            jnp.maximum(o2[0:64], o2[64:128]), jnp.maximum(o2[128:192], o2[192:256])
        )
        for half in range(2):
            u = tile * 2 + half
            v = jnp.maximum(m[:, half * 128 : half * 128 + 128] + b2c[...], 0.0)
            left = jnp.where(col64 == 0, 0.0, pltpu.roll(v, 1, 1))
            right = jnp.where(col64 == 31, 0.0, pltpu.roll(v, 127, 1))
            for dj, w in ((0, left), (1, v), (2, right)):
                pair = put(p3h, p3l, (3 + dj) * 64, 64, u, w)
                put_above(p3h, p3l, dj * 64, 64, u, w, pair, grp64)
                put_below(p3h, p3l, (6 + dj) * 64, 64, u, w, pair, grp64)
    final = []
    for tile in range(4):
        lanes = slice(tile * 256, tile * 256 + 256)
        first = dot(w3[...], p3h[:, lanes])
        o3 = first[0:128] + (first[128:256] + dot(w3[0:128, :], p3l[:, lanes]))
        o3 = jnp.maximum(o3, 0.0)
        for half in range(2):
            v = o3[:, half * 128 : half * 128 + 128] * k4c[...]
            final.append(jnp.sum(v, axis=0, keepdims=True))
    field = jnp.clip(jnp.concatenate(final, axis=0) + b4, -1.0, 1.0)
    m = jnp.where(4 * col < clen, field, -2.0)
    for step in (1, 2, 4, 8, 16):
        m = jnp.maximum(m, pltpu.roll(m, 128 - step, 1))
    counted = (col == 0) & (4 * (grp * 8 + sub) < qlen)
    score = jnp.sum(jnp.where(counted, m, 0.0), keepdims=True)
    number = ((jnp.full((8, 128), qlen, jnp.int32) + 3) >> 2).astype(F32)
    return jnp.broadcast_to(score, (8, 128)) / number


def kernel(
    q_ref, f_ref, cand_v, cand_s, qlen_ref, clen_ref,
    k1, b1, k2, b2, k3, b3, k4, b4,
    out_ref,
    frames, outgoing, landed, mid, x, qbuf, best, sq, w1, w2, w3, b2c, k4c,
    p1f, p1b, p2h, p2l, p3h, p3l, scores,
    f_sem, a_send, a_recv, b_send, b_recv, q_send, q_recv, s_send, s_recv,
):
    pb = lax.axis_index("pb")
    slab = lax.axis_index("slab")
    my_y = lax.div(pb, NZ * NC)
    my_z = lax.rem(lax.div(pb, NC), NZ)
    my_c = lax.rem(pb, NC)
    my_slot = my_c * NY + my_y

    def z_peer(step):
        z = lax.rem(my_z + step, NZ)
        return z, ((my_y * NZ + z) * NC + my_c, slab)

    def slot_peer(step):
        slot = lax.rem(my_slot + step, NSLOT)
        y, c = lax.rem(slot, NY), lax.div(slot, NY)
        return slot, ((y * NZ + my_z) * NC + c, slab)

    def x_peer(step):
        other = lax.rem(slab + step, NX)
        return other, (pb, other)

    barrier = pltpu.get_barrier_semaphore()
    for step in Z_ORDER:
        pl.semaphore_signal(barrier, inc=1, device_id=z_peer(step)[1], device_id_type=MESH)
    for step in range(1, NSLOT):
        pl.semaphore_signal(barrier, inc=1, device_id=slot_peer(step)[1], device_id_type=MESH)
    for step in range(1, NX):
        pl.semaphore_signal(barrier, inc=1, device_id=x_peer(step)[1], device_id_type=MESH)

    def fetch(chunk):
        return pltpu.make_async_copy(
            f_ref.at[pl.ds(chunk * SPER, SPER)], frames.at[chunk], f_sem.at[chunk]
        )

    for chunk in range(NCHUNK):
        fetch(chunk).start()

    n = iota((128, 128), 0)
    asks = ((n & 3) * NZ + (n >> 3)) * NC + ((n >> 2) & 1)
    order = hot(iota((128, 128), 1) == asks)
    wanted = jnp.broadcast_to(cand_v[pl.ds(slab, 1), :], (512, 128))
    select = dot_t(order, hot(iota((512, 128), 0) == wanted)).astype(BF)

    def gather(chunk):
        for s in range(SPER):
            rows = dot(select, frames[chunk, s])
            outgoing[chunk, s] = rows.reshape(NZ, NSLOT, 256).astype(BF)

    qi = iota((32, 32), 0)
    pick = hot(iota((32, 32), 1) == 4 * (qi & 7) + (qi >> 3))
    for r in range(9):
        qbuf[slab, r] = dot(pick, q_ref[r]).reshape(4, 8, 256).astype(BF)
    fetch(0).wait()
    gather(0)

    def send_a(chunk, step):
        z, device = z_peer(step)
        return pltpu.make_async_remote_copy(
            src_ref=outgoing.at[chunk, :, z],
            dst_ref=landed.at[chunk, my_z],
            send_sem=a_send.at[chunk, step],
            recv_sem=a_recv.at[chunk, my_z],
            device_id=device,
            device_id_type=MESH,
        )

    def recv_a(chunk, step):
        z, device = z_peer(step)
        return pltpu.make_async_remote_copy(
            src_ref=outgoing.at[chunk, :, z],
            dst_ref=landed.at[chunk, z],
            send_sem=a_send.at[chunk, step],
            recv_sem=a_recv.at[chunk, z],
            device_id=device,
            device_id_type=MESH,
        )

    def send_b(chunk, step):
        slot, device = slot_peer(step)
        return pltpu.make_async_remote_copy(
            src_ref=mid.at[chunk, slot],
            dst_ref=x.at[chunk, my_slot],
            send_sem=b_send.at[chunk, step],
            recv_sem=b_recv.at[chunk, my_slot],
            device_id=device,
            device_id_type=MESH,
        )

    def recv_b(chunk, step):
        slot, device = slot_peer(step)
        return pltpu.make_async_remote_copy(
            src_ref=mid.at[chunk, slot],
            dst_ref=x.at[chunk, slot],
            send_sem=b_send.at[chunk, step],
            recv_sem=b_recv.at[chunk, slot],
            device_id=device,
            device_id_type=MESH,
        )

    def x_copy(buffer, send, recv, step, arriving):
        other, device = x_peer(step)
        place = other if arriving else slab
        return pltpu.make_async_remote_copy(
            src_ref=buffer.at[slab],
            dst_ref=buffer.at[place],
            send_sem=send.at[step],
            recv_sem=recv.at[place],
            device_id=device,
            device_id_type=MESH,
        )

    pl.semaphore_wait(barrier, NZ - 1 + NSLOT - 1 + NX - 1)
    for step in Z_ORDER:
        send_a(0, step).start()
    for step in range(1, NX):
        x_copy(qbuf, q_send, q_recv, step, False).start()
    for chunk in range(1, NCHUNK):
        fetch(chunk).wait()
        gather(chunk)
        for step in Z_ORDER:
            send_a(chunk, step).start()

    prepare(k1, b1, k2, b2, k3, b3, k4, sq, w1, w2, w3, b2c, k4c, p1f, p1b, p3h, p3l)

    m = iota((128, 128), 0)
    source = (2 * (m & 7) + ((m >> 3) & 1)) * NSLOT + (m >> 4)
    shuffle = hot(iota((128, 128), 1) == source)

    def finish(chunk):
        for step in range(1, NSLOT):
            recv_b(chunk, step).wait_recv()
        gram_chunk(chunk, qbuf, x, best)

    for chunk in range(NCHUNK):
        for step in Z_ORDER:
            recv_a(chunk, step).wait_recv()
        for s in range(SPER):
            landed[chunk, my_z, s] = outgoing[chunk, s, my_z]
        for s in range(SPER):
            rows = dot(shuffle, landed[chunk, :, s].reshape(128, 256))
            mid[chunk, :, s] = rows.reshape(NSLOT, 2, 8, 256).astype(BF)
        for step in range(1, NSLOT):
            send_b(chunk, step).start()
        x[chunk, my_slot] = mid[chunk, my_slot]
        if chunk == 0:
            for step in range(1, NX):
                x_copy(qbuf, q_send, q_recv, step, True).wait_recv()
        else:
            finish(chunk - 1)
    finish(NCHUNK - 1)

    qlen = qlen_ref[0]
    clen = clen_ref[cand_s[slab, pb]]
    scores[slab] = refine(
        best, qlen, clen, b4[0], w1, w2, w3, b2c, k4c, p1f, p1b, p2h, p2l, p3h, p3l
    )
    for step in range(1, NX):
        x_copy(scores, s_send, s_recv, step, False).start()
    for chunk in range(NCHUNK):
        for step in Z_ORDER:
            send_a(chunk, step).wait_send()
        for step in range(1, NSLOT):
            send_b(chunk, step).wait_send()
    for step in range(1, NX):
        x_copy(qbuf, q_send, q_recv, step, False).wait_send()
    for step in range(1, NX):
        x_copy(scores, s_send, s_recv, step, True).wait_recv()
    for step in range(1, NX):
        x_copy(scores, s_send, s_recv, step, False).wait_send()
    where = iota((1, 128), 1)
    line = scores[0, 0:1]
    for other in range(1, NX):
        line = jnp.where(where == other, scores[other, 0:1], line)
    out_ref[...] = line[:, 0:4]


def compute_scratch():
    return [
        pltpu.VMEM((9, 128, 128), F32),
        pltpu.VMEM((128, 128), F32),
        pltpu.VMEM((512, 256), BF),
        pltpu.VMEM((512, 512), BF),
        pltpu.VMEM((256, 640), BF),
        pltpu.VMEM((64, 128), F32),
        pltpu.VMEM((128, 128), F32),
        pltpu.VMEM((384, 128), F32),
        pltpu.VMEM((256, 1024), BF),
        pltpu.VMEM((512, 1024), BF),
        pltpu.VMEM((512, 1024), BF),
        pltpu.VMEM((640, 1024), BF),
        pltpu.VMEM((640, 1024), BF),
    ]


def per_device(
    query_feats, frame_store, candidates, query_length, clip_length,
    kernel_one, bias_one, kernel_two, bias_two, kernel_three, bias_three, kernel_four, bias_four,
):
    vmem = pl.BlockSpec(memory_space=pltpu.VMEM)
    smem = pl.BlockSpec(memory_space=pltpu.SMEM)
    dma = pltpu.SemaphoreType.DMA
    pairs = candidates.T
    return pl.pallas_call(
        kernel,
        out_shape=jax.ShapeDtypeStruct((1, 4), F32),
        in_specs=[vmem, pl.BlockSpec(memory_space=pl.ANY), vmem, smem, smem, smem]
        + [vmem] * 7
        + [smem],
        out_specs=vmem,
        scratch_shapes=[
            pltpu.VMEM((NCHUNK, SPER, 512, 256), BF),
            pltpu.VMEM((NCHUNK, SPER, NZ, NSLOT, 256), BF),
            pltpu.VMEM((NCHUNK, NZ, SPER, NSLOT, 256), BF),
            pltpu.VMEM((NCHUNK, NSLOT, SPER, 2, 8, 256), BF),
            pltpu.VMEM((NCHUNK, NSLOT, SPER, 2, 8, 256), BF),
            pltpu.VMEM((NX, 9, 4, 8, 256), BF),
        ]
        + compute_scratch()
        + [
            pltpu.VMEM((NX, 8, 128), F32),
            dma((NCHUNK,)),
            dma((NCHUNK, NZ)),
            dma((NCHUNK, NZ)),
            dma((NCHUNK, NSLOT)),
            dma((NCHUNK, NSLOT)),
            dma((NX,)),
            dma((NX,)),
            dma((NX,)),
            dma((NX,)),
        ],
        compiler_params=pltpu.CompilerParams(collective_id=0, has_side_effects=True),
        name="score_pairs",
    )(
        query_feats[0].transpose(1, 0, 2),
        frame_store[:, 0].transpose(1, 0, 2),
        pairs,
        pairs,
        query_length,
        clip_length,
        kernel_one.reshape(9, 1, 32),
        bias_one.reshape(1, 32),
        kernel_two.reshape(288, 64),
        bias_two.reshape(1, 64),
        kernel_three.reshape(576, 128),
        bias_three.reshape(1, 128),
        kernel_four.reshape(1, 128),
        bias_four,
    )


def solution(mesh):
    placed = (
        P("pb", "slab", None, None),
        P(None, "pb", None, None),
        P(), P("pb"), P(), P(), P(), P(), P(), P(), P(), P(), P(),
    )
    return jax.shard_map(
        per_device, mesh=mesh, in_specs=placed, out_specs=P("pb", None), check_vma=False
    )
```

```python
import functools

import jax
import jax.numpy as jnp
from jax import lax
from jax.experimental import pallas as pl
from jax.experimental.pallas import tpu as pltpu
from jax.sharding import PartitionSpec as P

NY, NZ, NC, NX = 4, 16, 2, 4
NSLOT = NY * NC
CHUNKS = ((0, 2), (2, 5), (5, 9))
NEAR = 3
MESH = pl.DeviceIdType.MESH
BF = jnp.bfloat16
F32 = jnp.float32
Z_NEAR = tuple(step for far in range(1, NEAR + 1) for step in (far, NZ - far))
Z_FAR = (8,) + tuple(step for far in range(7, NEAR, -1) for step in (far, NZ - far))


def iota(shape, dim):
    return lax.broadcasted_iota(jnp.int32, shape, dim)


def dot(a, b):
    return lax.dot_general(a, b, (((1,), (0,)), ((), ())), preferred_element_type=F32)


def dot_t(a, b):
    return lax.dot_general(a, b, (((1,), (1,)), ((), ())), preferred_element_type=F32)


def hot(mask):
    return jnp.where(mask, 1.0, 0.0).astype(BF)


def halves(x):
    hi = x.astype(BF)
    lo = (x - hi.astype(F32)).astype(BF)
    return hi, lo


def prepare(k1, b1, k2, b2, k3, b3, k4, sq, w1, w2, w3, b2c, k4c, p1f, p1b, p3h, p3l):
    sq[...] = jnp.zeros_like(sq)
    for tap in range(9):
        sq[tap : tap + 1, 0:32] = k1[tap]
    sq[9:10, 0:32] = b1[...]
    hi, lo = halves(jnp.transpose(sq[...])[0:32])
    t = iota((128, 256), 0)
    k = iota((128, 256), 1)
    ti = jnp.where(t >= 3, 1, 0) + jnp.where(t >= 6, 1, 0)
    tj = t - 3 * ti
    for phase in range(16):
        row = 2 * (phase >> 3) + ((phase >> 1) & 1)
        col = 2 * ((phase >> 2) & 1) + (phase & 1)
        at = jnp.where(t == 9, 36, (row + ti) * 6 + col + tj)
        at = jnp.where(t > 9, -1000, at)
        both = hot((k == at) | (k == at + 48))
        last = hot(k == at + 96)
        w1[phase * 32 : phase * 32 + 32, :] = (dot(hi, both) + dot(lo, last)).astype(BF)
    w2[...] = jnp.zeros_like(w2)
    for ti in range(3):
        sq[...] = jnp.zeros_like(sq)
        sq[0:96, 0:64] = k2[ti * 96 : ti * 96 + 96, :]
        block = jnp.transpose(sq[...])[0:64]
        for a in range(2):
            for b in range(2):
                hi, lo = halves(block if b == 0 else pltpu.roll(block, 32, 1))
                lanes = slice((a + ti) * 128, (a + ti) * 128 + 128)
                row = (a * 2 + b) * 64
                w2[row : row + 64, lanes] = hi
                w2[256 + row : 256 + row + 64, lanes] = lo
    sq[...] = jnp.zeros_like(sq)
    sq[:, 0:64] = jnp.broadcast_to(b2[...], (128, 64))
    b2c[...] = jnp.transpose(sq[...])[0:64]
    for part in range(5):
        if part < 4:
            block = k3[part * 128 : part * 128 + 128, :]
        else:
            sq[...] = jnp.zeros_like(sq)
            sq[0:64, :] = k3[512:576, :]
            sq[64:65, :] = b3[...]
            block = sq[...]
        hi, lo = halves(jnp.transpose(block))
        w3[0:128, part * 128 : part * 128 + 128] = hi
        w3[128:256, part * 128 : part * 128 + 128] = lo
    k4c[...] = jnp.transpose(jnp.broadcast_to(k4[...], (128, 128)))
    p1b[144:256, :] = jnp.zeros((112, 1024), BF)
    ones = jnp.where(iota((16, 128), 0) == 4, 1.0, 0.0)
    for u in range(8):
        p1f[u * 48 + 32 : u * 48 + 48, :] = ones
    p3h[576:640, :] = hot(iota((64, 1024), 0) == 0)
    p3l[576:640, :] = jnp.zeros((64, 1024), BF)


def gram_chunk(chunk, qbuf, x, best):
    first, end = CHUNKS[chunk]
    p = iota((128, 128), 0)
    source = (2 * (p & 7) + (p >> 6)) * NSLOT + ((p >> 5) & 1) * NY + ((p >> 3) & 3)
    place = hot(iota((128, 128), 1) == source)
    right = [dot(place, x[:, s].reshape(128, 256)).astype(BF) for s in range(first, end)]
    right = jnp.concatenate(right, axis=0)
    for r in range(9):
        g = dot_t(qbuf[:, r].reshape(128, 256), right)
        m = g[:, 0:128]
        for s in range(1, end - first):
            m = jnp.maximum(m, g[:, s * 128 : s * 128 + 128])
        best[r] = m if chunk == 0 else jnp.maximum(best[r], m)


def refine(best, qlen, clen, b4, w1, w2, w3, b2c, k4c, p1f, p1b, p2h, p2l, p3h, p3l):
    lane = iota((8, 128), 1)
    sub = iota((8, 128), 0)
    grp = lane >> 5
    col = lane & 31
    total = best[0]
    for r in range(1, 9):
        total = total + best[r]
    total = total * (1.0 / 9.0)
    keep_col = (4 * col + grp) < clen
    sim = []
    for g in range(4):
        line = []
        for sg in range(4):
            at = (g * 4 + sg) * 8
            keep = keep_col & ((32 * g + 4 * sub + sg) < qlen)
            line.append(jnp.where(keep, total[at : at + 8], 0.0))
        sim.append(line)

    def up(x, nrow):
        y = pltpu.roll(x, 1, 0)
        z = jnp.where(grp == 0, 0.0, pltpu.roll(y, 32, 1))
        return jnp.where(sub == 0, z, y)

    def down(x, nrow):
        y = pltpu.roll(x, 7, 0)
        z = jnp.where(grp == 3, 0.0, pltpu.roll(y, 96, 1))
        return jnp.where(sub == 7, z, y)

    base = {}
    for sg in range(4):
        for rho in range(4):
            out = None
            for g in range(4):
                shift = ((g - rho) * 32) % 128
                piece = sim[g][sg] if shift == 0 else pltpu.roll(sim[g][sg], shift, 1)
                out = piece if out is None else jnp.where(grp == g, piece, out)
            base[sg, rho] = out
    rows = {}
    for rho in range(4):
        for sg in range(4):
            rows[sg, rho] = base[sg, rho]
        rows[-1, rho] = up(base[3, rho], 8)
        rows[4, rho] = down(base[0, rho], 8)
    for d in range(-1, 5):
        for e in range(-1, 5):
            if e == -1:
                v = jnp.where(col == 0, 0.0, pltpu.roll(rows[d, 3], 1, 1))
            elif e == 4:
                v = jnp.where(col == 31, 0.0, pltpu.roll(rows[d, 0], 127, 1))
            else:
                v = rows[d, e]
            p1f[pl.ds((d + 1) * 6 + e + 1, 8, stride=48), :] = v
    for u in range(8):
        hi, lo = halves(p1f[u * 48 : u * 48 + 48, :])
        lanes = slice(u * 128, u * 128 + 128)
        p1b[0:48, lanes] = hi
        p1b[48:96, lanes] = lo
        p1b[96:144, lanes] = hi

    def tall(x, n):
        return jnp.broadcast_to(x[0:1], (n, 128))

    grp32, col32 = tall(grp, 32), tall(col, 32)
    grp64, col64 = tall(grp, 64), tall(col, 64)

    def put(high, low, at, n, u, value):
        hi, lo = halves(value)
        high[at : at + n, u * 128 : u * 128 + 128] = hi
        low[at : at + n, u * 128 : u * 128 + 128] = lo
        return hi, lo

    def put_above(high, low, at, n, u, value, pair, groups):
        if u < 7:
            high[at : at + n, u * 128 + 128 : u * 128 + 256] = pair[0]
            low[at : at + n, u * 128 + 128 : u * 128 + 256] = pair[1]
        else:
            put(high, low, at, n, 0, jnp.where(groups == 0, 0.0, pltpu.roll(value, 32, 1)))

    def put_below(high, low, at, n, u, value, pair, groups):
        if u > 0:
            high[at : at + n, u * 128 - 128 : u * 128] = pair[0]
            low[at : at + n, u * 128 - 128 : u * 128] = pair[1]
        else:
            put(high, low, at, n, 7, jnp.where(groups == 3, 0.0, pltpu.roll(value, 96, 1)))

    for tile in range(4):
        o1 = dot(w1[...], p1b[:, tile * 256 : tile * 256 + 256])
        for ab in range(4):
            a, b = ab >> 1, ab & 1
            part = o1[ab * 128 : ab * 128 + 128]
            m = jnp.maximum(
                jnp.maximum(part[0:32], part[32:64]), jnp.maximum(part[64:96], part[96:128])
            )
            m = jnp.maximum(m, 0.0)
            for half in range(2):
                u = tile * 2 + half
                v = m[:, half * 128 : half * 128 + 128]
                if b == 1:
                    moved = jnp.where(col32 == 0, 0.0, pltpu.roll(v, 1, 1))
                    variants = ((2, v), (0, moved))
                else:
                    moved = jnp.where(col32 == 31, 0.0, pltpu.roll(v, 127, 1))
                    variants = ((1, v), (3, moved))
                for e, w in variants:
                    if a == 0:
                        pair = put(p2h, p2l, (4 + e) * 32, 32, u, w)
                        put_below(p2h, p2l, (12 + e) * 32, 32, u, w, pair, grp32)
                    else:
                        pair = put(p2h, p2l, (8 + e) * 32, 32, u, w)
                        put_above(p2h, p2l, e * 32, 32, u, w, pair, grp32)
    for tile in range(4):
        lanes = slice(tile * 256, tile * 256 + 256)
        first = dot(w2[...], p2h[:, lanes])
        o2 = first[0:256] + (first[256:512] + dot(w2[0:256, :], p2l[:, lanes]))
        m = jnp.maximum(
            jnp.maximum(o2[0:64], o2[64:128]), jnp.maximum(o2[128:192], o2[192:256])
        )
        for half in range(2):
            u = tile * 2 + half
            v = jnp.maximum(m[:, half * 128 : half * 128 + 128] + b2c[...], 0.0)
            left = jnp.where(col64 == 0, 0.0, pltpu.roll(v, 1, 1))
            right = jnp.where(col64 == 31, 0.0, pltpu.roll(v, 127, 1))
            for dj, w in ((0, left), (1, v), (2, right)):
                pair = put(p3h, p3l, (3 + dj) * 64, 64, u, w)
                put_above(p3h, p3l, dj * 64, 64, u, w, pair, grp64)
                put_below(p3h, p3l, (6 + dj) * 64, 64, u, w, pair, grp64)
    final = []
    for tile in range(4):
        lanes = slice(tile * 256, tile * 256 + 256)
        first = dot(w3[...], p3h[:, lanes])
        o3 = first[0:128] + (first[128:256] + dot(w3[0:128, :], p3l[:, lanes]))
        o3 = jnp.maximum(o3, 0.0)
        for half in range(2):
            v = o3[:, half * 128 : half * 128 + 128] * k4c[...]
            final.append(jnp.sum(v, axis=0, keepdims=True))
    field = jnp.clip(jnp.concatenate(final, axis=0) + b4, -1.0, 1.0)
    m = jnp.where(4 * col < clen, field, -2.0)
    for step in (1, 2, 4, 8, 16):
        m = jnp.maximum(m, pltpu.roll(m, 128 - step, 1))
    counted = (col == 0) & (4 * (grp * 8 + sub) < qlen)
    score = jnp.sum(jnp.where(counted, m, 0.0), keepdims=True)
    number = ((jnp.full((8, 128), qlen, jnp.int32) + 3) >> 2).astype(F32)
    return jnp.broadcast_to(score, (8, 128)) / number


def kernel(
    q_ref, f_ref, cand_v, cand_s, qlen_ref, clen_ref,
    k1, b1, k2, b2, k3, b3, k4, b4,
    out_ref,
    frames, outgoing, landed, mid, x, qbuf, best, sq, w1, w2, w3, b2c, k4c,
    p1f, p1b, p2h, p2l, p3h, p3l, scores,
    f_sem, a_send, a_recv, b_send, b_recv, q_send, q_recv, s_send, s_recv, below, above,
):
    pb = lax.axis_index("pb")
    slab = lax.axis_index("slab")
    my_y = lax.div(pb, NZ * NC)
    my_z = lax.rem(lax.div(pb, NC), NZ)
    my_c = lax.rem(pb, NC)
    my_slot = my_c * NY + my_y

    def z_peer(step):
        z = lax.rem(my_z + step, NZ)
        return z, ((my_y * NZ + z) * NC + my_c, slab)

    def slot_peer(step):
        slot = lax.rem(my_slot + step, NSLOT)
        y, c = lax.rem(slot, NY), lax.div(slot, NY)
        return slot, ((y * NZ + my_z) * NC + c, slab)

    def x_peer(step):
        other = lax.rem(slab + step, NX)
        return other, (pb, other)

    barrier = pltpu.get_barrier_semaphore()
    near = [z_peer(1), z_peer(NZ - 1)]
    near += [slot_peer(step) for step in range(1, NSLOT)]
    near += [x_peer(step) for step in range(1, NX)]
    for _, device in near:
        pl.semaphore_signal(barrier, inc=1, device_id=device, device_id_type=MESH)

    def fetch(chunk):
        first, end = CHUNKS[chunk]
        regions = pl.ds(first, end - first)
        return pltpu.make_async_copy(f_ref.at[regions], frames.at[regions], f_sem.at[chunk])

    chunks = range(len(CHUNKS))
    for chunk in chunks:
        fetch(chunk).start()

    n = iota((128, 128), 0)
    asks = (((n >> 4) & 3) * NZ + (n & 15)) * NC + (n >> 6)
    order = hot(iota((128, 128), 1) == asks)
    wanted = jnp.broadcast_to(cand_v[pl.ds(slab, 1), :], (512, 128))
    select = dot_t(order, hot(iota((512, 128), 0) == wanted)).astype(BF)

    def gather(chunk):
        fetch(chunk).wait()
        for s in range(*CHUNKS[chunk]):
            outgoing[:, s] = dot(select, frames[s]).reshape(NSLOT, NZ, 256).astype(BF)

    def send_b(chunk, step, arriving=False):
        first, end = CHUNKS[chunk]
        regions = pl.ds(first, end - first)
        slot, device = slot_peer(step)
        place = slot if arriving else my_slot
        return pltpu.make_async_remote_copy(
            src_ref=outgoing.at[slot, regions],
            dst_ref=landed.at[place, regions],
            send_sem=b_send.at[chunk, step],
            recv_sem=b_recv.at[chunk, place],
            device_id=device,
            device_id_type=MESH,
        )

    def send_a(chunk, step, arriving=False):
        first, end = CHUNKS[chunk]
        regions = pl.ds(first, end - first)
        z, device = z_peer(step)
        place = z if arriving else my_z
        return pltpu.make_async_remote_copy(
            src_ref=mid.at[z, regions],
            dst_ref=x.at[place, regions],
            send_sem=a_send.at[chunk, step],
            recv_sem=a_recv.at[chunk, place],
            device_id=device,
            device_id_type=MESH,
        )

    def x_copy(buffer, send, recv, step, arriving):
        other, device = x_peer(step)
        place = other if arriving else slab
        return pltpu.make_async_remote_copy(
            src_ref=buffer.at[slab],
            dst_ref=buffer.at[place],
            send_sem=send.at[step],
            recv_sem=recv.at[place],
            device_id=device,
            device_id_type=MESH,
        )

    def tell(k):
        if k <= 7:
            pl.semaphore_signal(
                below.at[k], inc=1, device_id=z_peer(1)[1], device_id_type=MESH
            )
        if k <= 6:
            pl.semaphore_signal(
                above.at[k], inc=1, device_id=z_peer(NZ - 1)[1], device_id_type=MESH
            )

    def hear(k):
        pl.semaphore_wait(below.at[k], 1)
        if k <= 6:
            pl.semaphore_wait(above.at[k], 1)
        tell(k + 1)

    m = iota((128, 128), 0)
    shuffle = hot(iota((128, 128), 1) == (m & 7) * NZ + (m >> 3))

    def turn(chunk):
        first, end = CHUNKS[chunk]
        landed[my_slot, first:end] = outgoing[my_slot, first:end]
        for step in range(1, NSLOT):
            send_b(chunk, step, True).wait_recv()
        for s in range(first, end):
            rows = dot(shuffle, landed[:, s].reshape(128, 256))
            mid[:, s] = rows.reshape(NZ, NSLOT, 256).astype(BF)

    gather(0)
    pl.semaphore_wait(barrier, len(near))
    tell(1)
    for step in range(1, NSLOT):
        send_b(0, step).start()
    qi = iota((32, 32), 0)
    pick = hot(iota((32, 32), 1) == 4 * (qi & 7) + (qi >> 3))
    for r in range(9):
        qbuf[slab, r] = dot(pick, q_ref[r]).reshape(4, 8, 256).astype(BF)
    for step in range(1, NX):
        x_copy(qbuf, q_send, q_recv, step, False).start()
    for chunk in chunks[1:]:
        gather(chunk)
        for step in range(1, NSLOT):
            send_b(chunk, step).start()
    for k in range(1, NEAR):
        hear(k)
    for chunk in chunks:
        turn(chunk)
        for step in Z_NEAR:
            send_a(chunk, step).start()
    for k in range(NEAR, 8):
        hear(k)
    for chunk in chunks:
        for step in Z_FAR:
            send_a(chunk, step).start()
        first, end = CHUNKS[chunk]
        x[my_z, first:end] = mid[my_z, first:end]

    prepare(k1, b1, k2, b2, k3, b3, k4, sq, w1, w2, w3, b2c, k4c, p1f, p1b, p3h, p3l)

    for step in range(1, NX):
        x_copy(qbuf, q_send, q_recv, step, True).wait_recv()
    for chunk in chunks:
        for step in Z_NEAR + Z_FAR:
            send_a(chunk, step, True).wait_recv()
        gram_chunk(chunk, qbuf, x, best)

    qlen = qlen_ref[0]
    clen = clen_ref[cand_s[slab, pb]]
    scores[slab] = refine(
        best, qlen, clen, b4[0], w1, w2, w3, b2c, k4c, p1f, p1b, p2h, p2l, p3h, p3l
    )
    for step in range(1, NX):
        x_copy(scores, s_send, s_recv, step, False).start()
    for chunk in chunks:
        for step in Z_NEAR + Z_FAR:
            send_a(chunk, step).wait_send()
        for step in range(1, NSLOT):
            send_b(chunk, step).wait_send()
    for step in range(1, NX):
        x_copy(qbuf, q_send, q_recv, step, False).wait_send()
    for step in range(1, NX):
        x_copy(scores, s_send, s_recv, step, True).wait_recv()
    for step in range(1, NX):
        x_copy(scores, s_send, s_recv, step, False).wait_send()
    where = iota((1, 128), 1)
    line = scores[0, 0:1]
    for other in range(1, NX):
        line = jnp.where(where == other, scores[other, 0:1], line)
    out_ref[...] = line[:, 0:4]


def compute_scratch():
    return [
        pltpu.VMEM((9, 128, 128), F32),
        pltpu.VMEM((128, 128), F32),
        pltpu.VMEM((512, 256), BF),
        pltpu.VMEM((512, 512), BF),
        pltpu.VMEM((256, 640), BF),
        pltpu.VMEM((64, 128), F32),
        pltpu.VMEM((128, 128), F32),
        pltpu.VMEM((384, 128), F32),
        pltpu.VMEM((256, 1024), BF),
        pltpu.VMEM((512, 1024), BF),
        pltpu.VMEM((512, 1024), BF),
        pltpu.VMEM((640, 1024), BF),
        pltpu.VMEM((640, 1024), BF),
    ]


def per_device(
    query_feats, frame_store, candidates, query_length, clip_length,
    kernel_one, bias_one, kernel_two, bias_two, kernel_three, bias_three, kernel_four, bias_four,
):
    vmem = pl.BlockSpec(memory_space=pltpu.VMEM)
    smem = pl.BlockSpec(memory_space=pltpu.SMEM)
    dma = pltpu.SemaphoreType.DMA
    pairs = candidates.T
    return pl.pallas_call(
        kernel,
        out_shape=jax.ShapeDtypeStruct((1, 4), F32),
        in_specs=[vmem, pl.BlockSpec(memory_space=pl.ANY), vmem, smem, smem, smem]
        + [vmem] * 7
        + [smem],
        out_specs=vmem,
        scratch_shapes=[
            pltpu.VMEM((9, 512, 256), BF),
            pltpu.VMEM((NSLOT, 9, NZ, 256), BF),
            pltpu.VMEM((NSLOT, 9, NZ, 256), BF),
            pltpu.VMEM((NZ, 9, NSLOT, 256), BF),
            pltpu.VMEM((NZ, 9, NSLOT, 256), BF),
            pltpu.VMEM((NX, 9, 4, 8, 256), BF),
        ]
        + compute_scratch()
        + [
            pltpu.VMEM((NX, 8, 128), F32),
            dma((len(CHUNKS),)),
            dma((len(CHUNKS), NZ)),
            dma((len(CHUNKS), NZ)),
            dma((len(CHUNKS), NSLOT)),
            dma((len(CHUNKS), NSLOT)),
            dma((NX,)),
            dma((NX,)),
            dma((NX,)),
            dma((NX,)),
            pltpu.SemaphoreType.REGULAR((8,)),
            pltpu.SemaphoreType.REGULAR((8,)),
        ],
        compiler_params=pltpu.CompilerParams(collective_id=0, has_side_effects=True),
        name="score_pairs",
    )(
        query_feats[0].transpose(1, 0, 2),
        frame_store[:, 0].transpose(1, 0, 2),
        pairs,
        pairs,
        query_length,
        clip_length,
        kernel_one.reshape(9, 1, 32),
        bias_one.reshape(1, 32),
        kernel_two.reshape(288, 64),
        bias_two.reshape(1, 64),
        kernel_three.reshape(576, 128),
        bias_three.reshape(1, 128),
        kernel_four.reshape(1, 128),
        bias_four,
    )


def solution(mesh):
    placed = (
        P("pb", "slab", None, None),
        P(None, "pb", None, None),
        P(), P("pb"), P(), P(), P(), P(), P(), P(), P(), P(), P(),
    )
    return jax.shard_map(
        per_device, mesh=mesh, in_specs=placed, out_specs=P("pb", None), check_vma=False
    )
```

```python
import functools

import jax
import jax.numpy as jnp
from jax import lax
from jax.experimental import pallas as pl
from jax.experimental.pallas import tpu as pltpu
from jax.sharding import PartitionSpec as P

NY, NZ, NC, NX = 4, 16, 2, 4
NSLOT = NY * NC
ALONG = ((0, 4),)
ACROSS = ((4, 7), (7, 9))
MESH = pl.DeviceIdType.MESH
BF = jnp.bfloat16
F32 = jnp.float32
Z_ORDER = (8, 7, 9, 6, 10, 5, 11, 4, 12, 3, 13, 2, 14, 1, 15)


def iota(shape, dim):
    return lax.broadcasted_iota(jnp.int32, shape, dim)


def dot(a, b):
    return lax.dot_general(a, b, (((1,), (0,)), ((), ())), preferred_element_type=F32)


def dot_t(a, b):
    return lax.dot_general(a, b, (((1,), (1,)), ((), ())), preferred_element_type=F32)


def hot(mask):
    return jnp.where(mask, 1.0, 0.0).astype(BF)


def halves(x):
    hi = x.astype(BF)
    lo = (x - hi.astype(F32)).astype(BF)
    return hi, lo


def prepare(k1, b1, k2, b2, k3, b3, k4, sq, w1, w2, w3, b2c, k4c, p1f, p1b, p3h, p3l):
    sq[...] = jnp.zeros_like(sq)
    for tap in range(9):
        sq[tap : tap + 1, 0:32] = k1[tap]
    sq[9:10, 0:32] = b1[...]
    hi, lo = halves(jnp.transpose(sq[...])[0:32])
    t = iota((128, 256), 0)
    k = iota((128, 256), 1)
    ti = jnp.where(t >= 3, 1, 0) + jnp.where(t >= 6, 1, 0)
    tj = t - 3 * ti
    for phase in range(16):
        row = 2 * (phase >> 3) + ((phase >> 1) & 1)
        col = 2 * ((phase >> 2) & 1) + (phase & 1)
        at = jnp.where(t == 9, 36, (row + ti) * 6 + col + tj)
        at = jnp.where(t > 9, -1000, at)
        both = hot((k == at) | (k == at + 48))
        last = hot(k == at + 96)
        w1[phase * 32 : phase * 32 + 32, :] = (dot(hi, both) + dot(lo, last)).astype(BF)
    w2[...] = jnp.zeros_like(w2)
    for ti in range(3):
        sq[...] = jnp.zeros_like(sq)
        sq[0:96, 0:64] = k2[ti * 96 : ti * 96 + 96, :]
        block = jnp.transpose(sq[...])[0:64]
        for a in range(2):
            for b in range(2):
                hi, lo = halves(block if b == 0 else pltpu.roll(block, 32, 1))
                lanes = slice((a + ti) * 128, (a + ti) * 128 + 128)
                row = (a * 2 + b) * 64
                w2[row : row + 64, lanes] = hi
                w2[256 + row : 256 + row + 64, lanes] = lo
    sq[...] = jnp.zeros_like(sq)
    sq[:, 0:64] = jnp.broadcast_to(b2[...], (128, 64))
    b2c[...] = jnp.transpose(sq[...])[0:64]
    for part in range(5):
        if part < 4:
            block = k3[part * 128 : part * 128 + 128, :]
        else:
            sq[...] = jnp.zeros_like(sq)
            sq[0:64, :] = k3[512:576, :]
            sq[64:65, :] = b3[...]
            block = sq[...]
        hi, lo = halves(jnp.transpose(block))
        w3[0:128, part * 128 : part * 128 + 128] = hi
        w3[128:256, part * 128 : part * 128 + 128] = lo
    k4c[...] = jnp.transpose(jnp.broadcast_to(k4[...], (128, 128)))
    p1b[144:256, :] = jnp.zeros((112, 1024), BF)
    ones = jnp.where(iota((16, 128), 0) == 4, 1.0, 0.0)
    for u in range(8):
        p1f[u * 48 + 32 : u * 48 + 48, :] = ones
    p3h[576:640, :] = hot(iota((64, 1024), 0) == 0)
    p3l[576:640, :] = jnp.zeros((64, 1024), BF)


def gram_chunk(chunk, right, qbuf, best):
    right = jnp.concatenate(right, axis=0)
    count = right.shape[0] // 128
    for r in range(9):
        g = dot_t(qbuf[:, r].reshape(128, 256), right)
        m = g[:, 0:128]
        for s in range(1, count):
            m = jnp.maximum(m, g[:, s * 128 : s * 128 + 128])
        best[r] = m if chunk == 0 else jnp.maximum(best[r], m)


def refine(best, qlen, clen, b4, w1, w2, w3, b2c, k4c, p1f, p1b, p2h, p2l, p3h, p3l):
    lane = iota((8, 128), 1)
    sub = iota((8, 128), 0)
    grp = lane >> 5
    col = lane & 31
    total = best[0]
    for r in range(1, 9):
        total = total + best[r]
    total = total * (1.0 / 9.0)
    keep_col = (4 * col + grp) < clen
    sim = []
    for g in range(4):
        line = []
        for sg in range(4):
            at = (g * 4 + sg) * 8
            keep = keep_col & ((32 * g + 4 * sub + sg) < qlen)
            line.append(jnp.where(keep, total[at : at + 8], 0.0))
        sim.append(line)

    def up(x, nrow):
        y = pltpu.roll(x, 1, 0)
        z = jnp.where(grp == 0, 0.0, pltpu.roll(y, 32, 1))
        return jnp.where(sub == 0, z, y)

    def down(x, nrow):
        y = pltpu.roll(x, 7, 0)
        z = jnp.where(grp == 3, 0.0, pltpu.roll(y, 96, 1))
        return jnp.where(sub == 7, z, y)

    base = {}
    for sg in range(4):
        for rho in range(4):
            out = None
            for g in range(4):
                shift = ((g - rho) * 32) % 128
                piece = sim[g][sg] if shift == 0 else pltpu.roll(sim[g][sg], shift, 1)
                out = piece if out is None else jnp.where(grp == g, piece, out)
            base[sg, rho] = out
    rows = {}
    for rho in range(4):
        for sg in range(4):
            rows[sg, rho] = base[sg, rho]
        rows[-1, rho] = up(base[3, rho], 8)
        rows[4, rho] = down(base[0, rho], 8)
    for d in range(-1, 5):
        for e in range(-1, 5):
            if e == -1:
                v = jnp.where(col == 0, 0.0, pltpu.roll(rows[d, 3], 1, 1))
            elif e == 4:
                v = jnp.where(col == 31, 0.0, pltpu.roll(rows[d, 0], 127, 1))
            else:
                v = rows[d, e]
            p1f[pl.ds((d + 1) * 6 + e + 1, 8, stride=48), :] = v
    for u in range(8):
        hi, lo = halves(p1f[u * 48 : u * 48 + 48, :])
        lanes = slice(u * 128, u * 128 + 128)
        p1b[0:48, lanes] = hi
        p1b[48:96, lanes] = lo
        p1b[96:144, lanes] = hi

    def tall(x, n):
        return jnp.broadcast_to(x[0:1], (n, 128))

    grp32, col32 = tall(grp, 32), tall(col, 32)
    grp64, col64 = tall(grp, 64), tall(col, 64)

    def put(high, low, at, n, u, value):
        hi, lo = halves(value)
        high[at : at + n, u * 128 : u * 128 + 128] = hi
        low[at : at + n, u * 128 : u * 128 + 128] = lo
        return hi, lo

    def put_above(high, low, at, n, u, value, pair, groups):
        if u < 7:
            high[at : at + n, u * 128 + 128 : u * 128 + 256] = pair[0]
            low[at : at + n, u * 128 + 128 : u * 128 + 256] = pair[1]
        else:
            put(high, low, at, n, 0, jnp.where(groups == 0, 0.0, pltpu.roll(value, 32, 1)))

    def put_below(high, low, at, n, u, value, pair, groups):
        if u > 0:
            high[at : at + n, u * 128 - 128 : u * 128] = pair[0]
            low[at : at + n, u * 128 - 128 : u * 128] = pair[1]
        else:
            put(high, low, at, n, 7, jnp.where(groups == 3, 0.0, pltpu.roll(value, 96, 1)))

    for tile in range(4):
        o1 = dot(w1[...], p1b[:, tile * 256 : tile * 256 + 256])
        for ab in range(4):
            a, b = ab >> 1, ab & 1
            part = o1[ab * 128 : ab * 128 + 128]
            m = jnp.maximum(
                jnp.maximum(part[0:32], part[32:64]), jnp.maximum(part[64:96], part[96:128])
            )
            m = jnp.maximum(m, 0.0)
            for half in range(2):
                u = tile * 2 + half
                v = m[:, half * 128 : half * 128 + 128]
                if b == 1:
                    moved = jnp.where(col32 == 0, 0.0, pltpu.roll(v, 1, 1))
                    variants = ((2, v), (0, moved))
                else:
                    moved = jnp.where(col32 == 31, 0.0, pltpu.roll(v, 127, 1))
                    variants = ((1, v), (3, moved))
                for e, w in variants:
                    if a == 0:
                        pair = put(p2h, p2l, (4 + e) * 32, 32, u, w)
                        put_below(p2h, p2l, (12 + e) * 32, 32, u, w, pair, grp32)
                    else:
                        pair = put(p2h, p2l, (8 + e) * 32, 32, u, w)
                        put_above(p2h, p2l, e * 32, 32, u, w, pair, grp32)
    for tile in range(4):
        lanes = slice(tile * 256, tile * 256 + 256)
        first = dot(w2[...], p2h[:, lanes])
        o2 = first[0:256] + (first[256:512] + dot(w2[0:256, :], p2l[:, lanes]))
        m = jnp.maximum(
            jnp.maximum(o2[0:64], o2[64:128]), jnp.maximum(o2[128:192], o2[192:256])
        )
        for half in range(2):
            u = tile * 2 + half
            v = jnp.maximum(m[:, half * 128 : half * 128 + 128] + b2c[...], 0.0)
            left = jnp.where(col64 == 0, 0.0, pltpu.roll(v, 1, 1))
            right = jnp.where(col64 == 31, 0.0, pltpu.roll(v, 127, 1))
            for dj, w in ((0, left), (1, v), (2, right)):
                pair = put(p3h, p3l, (3 + dj) * 64, 64, u, w)
                put_above(p3h, p3l, dj * 64, 64, u, w, pair, grp64)
                put_below(p3h, p3l, (6 + dj) * 64, 64, u, w, pair, grp64)
    final = []
    for tile in range(4):
        lanes = slice(tile * 256, tile * 256 + 256)
        first = dot(w3[...], p3h[:, lanes])
        o3 = first[0:128] + (first[128:256] + dot(w3[0:128, :], p3l[:, lanes]))
        o3 = jnp.maximum(o3, 0.0)
        for half in range(2):
            v = o3[:, half * 128 : half * 128 + 128] * k4c[...]
            final.append(jnp.sum(v, axis=0, keepdims=True))
    field = jnp.clip(jnp.concatenate(final, axis=0) + b4, -1.0, 1.0)
    m = jnp.where(4 * col < clen, field, -2.0)
    for step in (1, 2, 4, 8, 16):
        m = jnp.maximum(m, pltpu.roll(m, 128 - step, 1))
    counted = (col == 0) & (4 * (grp * 8 + sub) < qlen)
    score = jnp.sum(jnp.where(counted, m, 0.0), keepdims=True)
    number = ((jnp.full((8, 128), qlen, jnp.int32) + 3) >> 2).astype(F32)
    return jnp.broadcast_to(score, (8, 128)) / number


def kernel(*refs):
    operands, refs = refs[:14], refs[14:]
    out_ref, refs = refs[0], refs[1:]
    copies, refs = refs[:14], refs[14:]
    (
        zout, zin, smid, xs, sout, sin, zmid, xz, qbuf, best, sq, w1, w2, w3, b2c, k4c,
        p1f, p1b, p2h, p2l, p3h, p3l, scores,
        in_sem, f_sem, a_send, a_recv, b_send, b_recv, q_send, q_recv, s_send, s_recv,
    ) = refs
    q_ref, frames, cand_v, cand_s, qlen_ref, clen_ref, k1, b1, k2, b2, k3, b3, k4, b4 = copies
    pb = lax.axis_index("pb")
    slab = lax.axis_index("slab")
    my_y = lax.div(pb, NZ * NC)
    my_z = lax.rem(lax.div(pb, NC), NZ)
    my_c = lax.rem(pb, NC)
    my_slot = my_c * NY + my_y

    def z_peer(step):
        z = lax.rem(my_z + step, NZ)
        return z, ((my_y * NZ + z) * NC + my_c, slab)

    def slot_peer(step):
        slot = lax.rem(my_slot + step, NSLOT)
        y, c = lax.rem(slot, NY), lax.div(slot, NY)
        return slot, ((y * NZ + my_z) * NC + c, slab)

    def x_peer(step):
        other = lax.rem(slab + step, NX)
        return other, (pb, other)

    barrier = pltpu.get_barrier_semaphore()
    peers = [z_peer(step) for step in Z_ORDER]
    peers += [slot_peer(step) for step in range(1, NSLOT)]
    peers += [x_peer(step) for step in range(1, NX)]
    for _, device in peers:
        pl.semaphore_signal(barrier, inc=1, device_id=device, device_id_type=MESH)

    chunks = ALONG + ACROSS

    def fetch(chunk):
        first, end = chunks[chunk]
        regions = pl.ds(first, end - first)
        return pltpu.make_async_copy(
            operands[1].at[regions], frames.at[regions], f_sem.at[chunk]
        )

    def bring(i):
        return pltpu.make_async_copy(operands[i], copies[i], in_sem.at[i])

    bring(2).start()
    for chunk in range(len(chunks)):
        fetch(chunk).start()
    others = (0, 3, 4, 5, 6, 7, 8, 9, 10, 11, 12, 13)
    for i in others:
        bring(i).start()

    n = iota((128, 128), 0)
    lane = iota((128, 128), 1)
    zs = hot(lane == ((n & 3) * NZ + (n >> 3)) * NC + ((n >> 2) & 1))
    sz = hot(lane == (((n >> 4) & 3) * NZ + (n & 15)) * NC + (n >> 6))
    bring(2).wait()
    wanted = jnp.broadcast_to(cand_v[pl.ds(slab, 1), :], (512, 128))
    wanted = hot(iota((512, 128), 0) == wanted)

    def z_copy(chunk, step, src, dst, arriving=False):
        first, end = chunks[chunk]
        regions = pl.ds(first, end - first)
        z, device = z_peer(step)
        place = z if arriving else my_z
        return pltpu.make_async_remote_copy(
            src_ref=src.at[z, regions],
            dst_ref=dst.at[place, regions],
            send_sem=a_send.at[chunk, step],
            recv_sem=a_recv.at[chunk, place],
            device_id=device,
            device_id_type=MESH,
        )

    def s_copy(chunk, step, src, dst, arriving=False):
        first, end = chunks[chunk]
        regions = pl.ds(first, end - first)
        slot, device = slot_peer(step)
        place = slot if arriving else my_slot
        return pltpu.make_async_remote_copy(
            src_ref=src.at[slot, regions],
            dst_ref=dst.at[place, regions],
            send_sem=b_send.at[chunk, step],
            recv_sem=b_recv.at[chunk, place],
            device_id=device,
            device_id_type=MESH,
        )

    def x_copy(buffer, send, recv, step, arriving):
        other, device = x_peer(step)
        place = other if arriving else slab
        return pltpu.make_async_remote_copy(
            src_ref=buffer.at[slab],
            dst_ref=buffer.at[place],
            send_sem=send.at[step],
            recv_sem=recv.at[place],
            device_id=device,
            device_id_type=MESH,
        )

    def z_start(chunk, src, dst):
        for step in Z_ORDER:
            z_copy(chunk, step, src, dst).start()
        first, end = chunks[chunk]
        dst[my_z, first:end] = src[my_z, first:end]

    def s_start(chunk, src, dst):
        for step in range(1, NSLOT):
            s_copy(chunk, step, src, dst).start()
        first, end = chunks[chunk]
        dst[my_slot, first:end] = src[my_slot, first:end]

    def z_wait(chunk, src, dst):
        for step in Z_ORDER:
            z_copy(chunk, step, src, dst, True).wait_recv()

    def s_wait(chunk, src, dst):
        for step in range(1, NSLOT):
            s_copy(chunk, step, src, dst, True).wait_recv()

    along = range(len(ALONG))
    across = range(len(ALONG), len(chunks))

    def gather_along(chunk):
        fetch(chunk).wait()
        for s in range(*chunks[chunk]):
            zout[:, s] = dot(by_z, frames[s]).reshape(NZ, NSLOT, 256).astype(BF)

    def gather_across(chunk):
        fetch(chunk).wait()
        for s in range(*chunks[chunk]):
            sout[:, s] = dot(by_slot, frames[s]).reshape(NSLOT, NZ, 256).astype(BF)

    by_z = dot_t(zs, wanted).astype(BF)
    for chunk in along:
        gather_along(chunk)
    by_slot = dot_t(sz, wanted).astype(BF)
    bring(0).wait()
    qi = iota((32, 32), 0)
    pick = hot(iota((32, 32), 1) == 4 * (qi & 7) + (qi >> 3))
    for r in range(9):
        qbuf[slab, r] = dot(pick, q_ref[r]).reshape(4, 8, 256).astype(BF)
    for chunk in across:
        gather_across(chunk)

    pl.semaphore_wait(barrier, len(peers))
    for chunk in along:
        z_start(chunk, zout, zin)
    for chunk in across:
        s_start(chunk, sout, sin)
    for step in range(1, NX):
        x_copy(qbuf, q_send, q_recv, step, False).start()
    for i in others[1:]:
        bring(i).wait()

    to_z = hot(lane == (n & 7) * NZ + (n >> 3))
    to_slot = hot(lane == (2 * (n & 7) + ((n >> 3) & 1)) * NSLOT + (n >> 4))
    place = hot(
        lane == (2 * (n & 7) + (n >> 6)) * NSLOT + ((n >> 5) & 1) * NY + ((n >> 3) & 3)
    )
    for chunk in across:
        s_wait(chunk, sout, sin)
        for s in range(*chunks[chunk]):
            rows = dot(to_z, sin[:, s].reshape(128, 256))
            zmid[:, s] = rows.reshape(NZ, NSLOT, 256).astype(BF)
        z_start(chunk, zmid, xz)

    prepare(k1, b1, k2, b2, k3, b3, k4, sq, w1, w2, w3, b2c, k4c, p1f, p1b, p3h, p3l)

    for chunk in along:
        z_wait(chunk, zout, zin)
        for s in range(*chunks[chunk]):
            rows = dot(to_slot, zin[:, s].reshape(128, 256))
            smid[:, s] = rows.reshape(NSLOT, 2, 8, 256).astype(BF)
        s_start(chunk, smid, xs)
    for step in range(1, NX):
        x_copy(qbuf, q_send, q_recv, step, True).wait_recv()
    for chunk in along:
        s_wait(chunk, smid, xs)
        right = [
            xs[:, s, e].reshape(64, 256) for s in range(*chunks[chunk]) for e in range(2)
        ]
        gram_chunk(chunk, right, qbuf, best)
    for chunk in across:
        z_wait(chunk, zmid, xz)
        right = [
            dot(place, xz[:, s].reshape(128, 256)).astype(BF) for s in range(*chunks[chunk])
        ]
        gram_chunk(chunk, right, qbuf, best)

    qlen = qlen_ref[0]
    clen = clen_ref[cand_s[slab, pb]]
    scores[slab] = refine(
        best, qlen, clen, b4[0], w1, w2, w3, b2c, k4c, p1f, p1b, p2h, p2l, p3h, p3l
    )
    for step in range(1, NX):
        x_copy(scores, s_send, s_recv, step, False).start()
    for chunk in range(len(chunks)):
        line, pair = ((zout, zin), (smid, xs)) if chunk in along else ((zmid, xz), (sout, sin))
        for step in Z_ORDER:
            z_copy(chunk, step, *line).wait_send()
        for step in range(1, NSLOT):
            s_copy(chunk, step, *pair).wait_send()
    for step in range(1, NX):
        x_copy(qbuf, q_send, q_recv, step, False).wait_send()
    for step in range(1, NX):
        x_copy(scores, s_send, s_recv, step, True).wait_recv()
    for step in range(1, NX):
        x_copy(scores, s_send, s_recv, step, False).wait_send()
    where = iota((1, 128), 1)
    line = scores[0, 0:1]
    for other in range(1, NX):
        line = jnp.where(where == other, scores[other, 0:1], line)
    out_ref[...] = line[:, 0:4]


def compute_scratch():
    return [
        pltpu.VMEM((9, 128, 128), F32),
        pltpu.VMEM((128, 128), F32),
        pltpu.VMEM((512, 256), BF),
        pltpu.VMEM((512, 512), BF),
        pltpu.VMEM((256, 640), BF),
        pltpu.VMEM((64, 128), F32),
        pltpu.VMEM((128, 128), F32),
        pltpu.VMEM((384, 128), F32),
        pltpu.VMEM((256, 1024), BF),
        pltpu.VMEM((512, 1024), BF),
        pltpu.VMEM((512, 1024), BF),
        pltpu.VMEM((640, 1024), BF),
        pltpu.VMEM((640, 1024), BF),
    ]


def per_device(
    query_feats, frame_store, candidates, query_length, clip_length,
    kernel_one, bias_one, kernel_two, bias_two, kernel_three, bias_three, kernel_four, bias_four,
):
    vmem = pl.BlockSpec(memory_space=pltpu.VMEM)
    dma = pltpu.SemaphoreType.DMA
    count = len(ALONG + ACROSS)
    pairs = candidates.T
    by_z = pltpu.VMEM((NZ, 9, NSLOT, 256), BF)
    by_slot = pltpu.VMEM((NSLOT, 9, NZ, 256), BF)
    to_gram = pltpu.VMEM((NSLOT, 9, 2, 8, 256), BF)
    return pl.pallas_call(
        kernel,
        out_shape=jax.ShapeDtypeStruct((1, 4), F32),
        in_specs=[pl.BlockSpec(memory_space=pl.ANY)] * 14,
        out_specs=vmem,
        scratch_shapes=[
            pltpu.VMEM((9, 32, 256), BF),
            pltpu.VMEM((9, 512, 256), BF),
            pltpu.VMEM((4, 128), jnp.int32),
            pltpu.SMEM((4, 128), jnp.int32),
            pltpu.SMEM((1,), jnp.int32),
            pltpu.SMEM((512,), jnp.int32),
            pltpu.VMEM((9, 1, 32), F32),
            pltpu.VMEM((1, 32), F32),
            pltpu.VMEM((288, 64), F32),
            pltpu.VMEM((1, 64), F32),
            pltpu.VMEM((576, 128), F32),
            pltpu.VMEM((1, 128), F32),
            pltpu.VMEM((1, 128), F32),
            pltpu.SMEM((1,), F32),
            by_z, by_z, to_gram, to_gram, by_slot, by_slot, by_z, by_z,
            pltpu.VMEM((NX, 9, 4, 8, 256), BF),
        ]
        + compute_scratch()
        + [
            pltpu.VMEM((NX, 8, 128), F32),
            dma((14,)),
            dma((count,)),
            dma((count, NZ)),
            dma((count, NZ)),
            dma((count, NSLOT)),
            dma((count, NSLOT)),
            dma((NX,)),
            dma((NX,)),
            dma((NX,)),
            dma((NX,)),
        ],
        compiler_params=pltpu.CompilerParams(collective_id=0, has_side_effects=True),
        name="score_pairs",
    )(
        query_feats[0].transpose(1, 0, 2),
        frame_store[:, 0].transpose(1, 0, 2),
        pairs,
        pairs,
        query_length,
        clip_length,
        kernel_one.reshape(9, 1, 32),
        bias_one.reshape(1, 32),
        kernel_two.reshape(288, 64),
        bias_two.reshape(1, 64),
        kernel_three.reshape(576, 128),
        bias_three.reshape(1, 128),
        kernel_four.reshape(1, 128),
        bias_four,
    )


def solution(mesh):
    placed = (
        P("pb", "slab", None, None),
        P(None, "pb", None, None),
        P(), P("pb"), P(), P(), P(), P(), P(), P(), P(), P(), P(),
    )
    return jax.shard_map(
        per_device, mesh=mesh, in_specs=placed, out_specs=P("pb", None), check_vma=False
    )
```

```python
import functools

import jax
import jax.numpy as jnp
from jax import lax
from jax.experimental import pallas as pl
from jax.experimental.pallas import tpu as pltpu
from jax.sharding import PartitionSpec as P

NY, NZ, NC, NX = 4, 16, 2, 4
NSLOT = NY * NC
ALONG = ((0, 5),)
ACROSS = ((5, 9),)
MESH = pl.DeviceIdType.MESH
BF = jnp.bfloat16
F32 = jnp.float32
Z_ORDER = (8, 7, 9, 6, 10, 5, 11, 4, 12, 3, 13, 2, 14, 1, 15)


def iota(shape, dim):
    return lax.broadcasted_iota(jnp.int32, shape, dim)


def dot(a, b):
    return lax.dot_general(a, b, (((1,), (0,)), ((), ())), preferred_element_type=F32)


def dot_t(a, b):
    return lax.dot_general(a, b, (((1,), (1,)), ((), ())), preferred_element_type=F32)


def hot(mask):
    return jnp.where(mask, 1.0, 0.0).astype(BF)


def halves(x):
    hi = x.astype(BF)
    lo = (x - hi.astype(F32)).astype(BF)
    return hi, lo


def prepare(k1, b1, k2, b2, k3, b3, k4, sq, w1, w2, w3, b2c, k4c, p1f, p1b, p3h, p3l):
    sq[...] = jnp.zeros_like(sq)
    for tap in range(9):
        sq[tap : tap + 1, 0:32] = k1[tap]
    sq[9:10, 0:32] = b1[...]
    hi, lo = halves(jnp.transpose(sq[...])[0:32])
    t = iota((128, 256), 0)
    k = iota((128, 256), 1)
    ti = jnp.where(t >= 3, 1, 0) + jnp.where(t >= 6, 1, 0)
    tj = t - 3 * ti
    for phase in range(16):
        row = 2 * (phase >> 3) + ((phase >> 1) & 1)
        col = 2 * ((phase >> 2) & 1) + (phase & 1)
        at = jnp.where(t == 9, 36, (row + ti) * 6 + col + tj)
        at = jnp.where(t > 9, -1000, at)
        both = hot((k == at) | (k == at + 48))
        last = hot(k == at + 96)
        w1[phase * 32 : phase * 32 + 32, :] = (dot(hi, both) + dot(lo, last)).astype(BF)
    w2[...] = jnp.zeros_like(w2)
    for ti in range(3):
        sq[...] = jnp.zeros_like(sq)
        sq[0:96, 0:64] = k2[ti * 96 : ti * 96 + 96, :]
        block = jnp.transpose(sq[...])[0:64]
        for a in range(2):
            for b in range(2):
                hi, lo = halves(block if b == 0 else pltpu.roll(block, 32, 1))
                lanes = slice((a + ti) * 128, (a + ti) * 128 + 128)
                row = (a * 2 + b) * 64
                w2[row : row + 64, lanes] = hi
                w2[256 + row : 256 + row + 64, lanes] = lo
    sq[...] = jnp.zeros_like(sq)
    sq[:, 0:64] = jnp.broadcast_to(b2[...], (128, 64))
    b2c[...] = jnp.transpose(sq[...])[0:64]
    for part in range(5):
        if part < 4:
            block = k3[part * 128 : part * 128 + 128, :]
        else:
            sq[...] = jnp.zeros_like(sq)
            sq[0:64, :] = k3[512:576, :]
            sq[64:65, :] = b3[...]
            block = sq[...]
        hi, lo = halves(jnp.transpose(block))
        w3[0:128, part * 128 : part * 128 + 128] = hi
        w3[128:256, part * 128 : part * 128 + 128] = lo
    k4c[...] = jnp.transpose(jnp.broadcast_to(k4[...], (128, 128)))
    p1b[144:256, :] = jnp.zeros((112, 1024), BF)
    ones = jnp.where(iota((16, 128), 0) == 4, 1.0, 0.0)
    for u in range(8):
        p1f[u * 48 + 32 : u * 48 + 48, :] = ones
    p3h[576:640, :] = hot(iota((64, 1024), 0) == 0)
    p3l[576:640, :] = jnp.zeros((64, 1024), BF)


def gram_chunk(chunk, right, qbuf, best):
    right = jnp.concatenate(right, axis=0)
    count = right.shape[0] // 128
    for r in range(9):
        g = dot_t(qbuf[:, r].reshape(128, 256), right)
        m = g[:, 0:128]
        for s in range(1, count):
            m = jnp.maximum(m, g[:, s * 128 : s * 128 + 128])
        best[r] = m if chunk == 0 else jnp.maximum(best[r], m)


def refine(best, qlen, clen, b4, w1, w2, w3, b2c, k4c, p1f, p1b, p2h, p2l, p3h, p3l):
    lane = iota((8, 128), 1)
    sub = iota((8, 128), 0)
    grp = lane >> 5
    col = lane & 31
    total = best[0]
    for r in range(1, 9):
        total = total + best[r]
    total = total * (1.0 / 9.0)
    keep_col = (4 * col + grp) < clen
    sim = []
    for g in range(4):
        line = []
        for sg in range(4):
            at = (g * 4 + sg) * 8
            keep = keep_col & ((32 * g + 4 * sub + sg) < qlen)
            line.append(jnp.where(keep, total[at : at + 8], 0.0))
        sim.append(line)

    def up(x, nrow):
        y = pltpu.roll(x, 1, 0)
        z = jnp.where(grp == 0, 0.0, pltpu.roll(y, 32, 1))
        return jnp.where(sub == 0, z, y)

    def down(x, nrow):
        y = pltpu.roll(x, 7, 0)
        z = jnp.where(grp == 3, 0.0, pltpu.roll(y, 96, 1))
        return jnp.where(sub == 7, z, y)

    base = {}
    for sg in range(4):
        for rho in range(4):
            out = None
            for g in range(4):
                shift = ((g - rho) * 32) % 128
                piece = sim[g][sg] if shift == 0 else pltpu.roll(sim[g][sg], shift, 1)
                out = piece if out is None else jnp.where(grp == g, piece, out)
            base[sg, rho] = out
    rows = {}
    for rho in range(4):
        for sg in range(4):
            rows[sg, rho] = base[sg, rho]
        rows[-1, rho] = up(base[3, rho], 8)
        rows[4, rho] = down(base[0, rho], 8)
    for d in range(-1, 5):
        for e in range(-1, 5):
            if e == -1:
                v = jnp.where(col == 0, 0.0, pltpu.roll(rows[d, 3], 1, 1))
            elif e == 4:
                v = jnp.where(col == 31, 0.0, pltpu.roll(rows[d, 0], 127, 1))
            else:
                v = rows[d, e]
            p1f[pl.ds((d + 1) * 6 + e + 1, 8, stride=48), :] = v
    for u in range(8):
        hi, lo = halves(p1f[u * 48 : u * 48 + 48, :])
        lanes = slice(u * 128, u * 128 + 128)
        p1b[0:48, lanes] = hi
        p1b[48:96, lanes] = lo
        p1b[96:144, lanes] = hi

    def tall(x, n):
        return jnp.broadcast_to(x[0:1], (n, 128))

    grp32, col32 = tall(grp, 32), tall(col, 32)
    grp64, col64 = tall(grp, 64), tall(col, 64)

    def put(high, low, at, n, u, value):
        hi, lo = halves(value)
        high[at : at + n, u * 128 : u * 128 + 128] = hi
        low[at : at + n, u * 128 : u * 128 + 128] = lo
        return hi, lo

    def put_above(high, low, at, n, u, value, pair, groups):
        if u < 7:
            high[at : at + n, u * 128 + 128 : u * 128 + 256] = pair[0]
            low[at : at + n, u * 128 + 128 : u * 128 + 256] = pair[1]
        else:
            put(high, low, at, n, 0, jnp.where(groups == 0, 0.0, pltpu.roll(value, 32, 1)))

    def put_below(high, low, at, n, u, value, pair, groups):
        if u > 0:
            high[at : at + n, u * 128 - 128 : u * 128] = pair[0]
            low[at : at + n, u * 128 - 128 : u * 128] = pair[1]
        else:
            put(high, low, at, n, 7, jnp.where(groups == 3, 0.0, pltpu.roll(value, 96, 1)))

    for tile in range(4):
        o1 = dot(w1[...], p1b[:, tile * 256 : tile * 256 + 256])
        for ab in range(4):
            a, b = ab >> 1, ab & 1
            part = o1[ab * 128 : ab * 128 + 128]
            m = jnp.maximum(
                jnp.maximum(part[0:32], part[32:64]), jnp.maximum(part[64:96], part[96:128])
            )
            m = jnp.maximum(m, 0.0)
            for half in range(2):
                u = tile * 2 + half
                v = m[:, half * 128 : half * 128 + 128]
                if b == 1:
                    moved = jnp.where(col32 == 0, 0.0, pltpu.roll(v, 1, 1))
                    variants = ((2, v), (0, moved))
                else:
                    moved = jnp.where(col32 == 31, 0.0, pltpu.roll(v, 127, 1))
                    variants = ((1, v), (3, moved))
                for e, w in variants:
                    if a == 0:
                        pair = put(p2h, p2l, (4 + e) * 32, 32, u, w)
                        put_below(p2h, p2l, (12 + e) * 32, 32, u, w, pair, grp32)
                    else:
                        pair = put(p2h, p2l, (8 + e) * 32, 32, u, w)
                        put_above(p2h, p2l, e * 32, 32, u, w, pair, grp32)
    for tile in range(4):
        lanes = slice(tile * 256, tile * 256 + 256)
        first = dot(w2[...], p2h[:, lanes])
        o2 = first[0:256] + (first[256:512] + dot(w2[0:256, :], p2l[:, lanes]))
        m = jnp.maximum(
            jnp.maximum(o2[0:64], o2[64:128]), jnp.maximum(o2[128:192], o2[192:256])
        )
        for half in range(2):
            u = tile * 2 + half
            v = jnp.maximum(m[:, half * 128 : half * 128 + 128] + b2c[...], 0.0)
            left = jnp.where(col64 == 0, 0.0, pltpu.roll(v, 1, 1))
            right = jnp.where(col64 == 31, 0.0, pltpu.roll(v, 127, 1))
            for dj, w in ((0, left), (1, v), (2, right)):
                pair = put(p3h, p3l, (3 + dj) * 64, 64, u, w)
                put_above(p3h, p3l, dj * 64, 64, u, w, pair, grp64)
                put_below(p3h, p3l, (6 + dj) * 64, 64, u, w, pair, grp64)
    final = []
    for tile in range(4):
        lanes = slice(tile * 256, tile * 256 + 256)
        first = dot(w3[...], p3h[:, lanes])
        o3 = first[0:128] + (first[128:256] + dot(w3[0:128, :], p3l[:, lanes]))
        o3 = jnp.maximum(o3, 0.0)
        for half in range(2):
            v = o3[:, half * 128 : half * 128 + 128] * k4c[...]
            final.append(jnp.sum(v, axis=0, keepdims=True))
    field = jnp.clip(jnp.concatenate(final, axis=0) + b4, -1.0, 1.0)
    m = jnp.where(4 * col < clen, field, -2.0)
    for step in (1, 2, 4, 8, 16):
        m = jnp.maximum(m, pltpu.roll(m, 128 - step, 1))
    counted = (col == 0) & (4 * (grp * 8 + sub) < qlen)
    score = jnp.sum(jnp.where(counted, m, 0.0), keepdims=True)
    number = ((jnp.full((8, 128), qlen, jnp.int32) + 3) >> 2).astype(F32)
    return jnp.broadcast_to(score, (8, 128)) / number


def kernel(*refs):
    operands, refs = refs[:14], refs[14:]
    out_ref, refs = refs[0], refs[1:]
    copies, refs = refs[:14], refs[14:]
    (
        zout, zin, smid, xs, sout, sin, zmid, xz, qbuf, best, sq, w1, w2, w3, b2c, k4c,
        p1f, p1b, p2h, p2l, p3h, p3l, scores,
        in_sem, f_sem, a_send, a_recv, b_send, b_recv, q_send, q_recv, s_send, s_recv,
    ) = refs
    q_ref, frames, cand_v, cand_s, qlen_ref, clen_ref, k1, b1, k2, b2, k3, b3, k4, b4 = copies
    pb = lax.axis_index("pb")
    slab = lax.axis_index("slab")
    my_y = lax.div(pb, NZ * NC)
    my_z = lax.rem(lax.div(pb, NC), NZ)
    my_c = lax.rem(pb, NC)
    my_slot = my_c * NY + my_y

    def z_peer(step):
        z = lax.rem(my_z + step, NZ)
        return z, ((my_y * NZ + z) * NC + my_c, slab)

    def slot_peer(step):
        slot = lax.rem(my_slot + step, NSLOT)
        y, c = lax.rem(slot, NY), lax.div(slot, NY)
        return slot, ((y * NZ + my_z) * NC + c, slab)

    def x_peer(step):
        other = lax.rem(slab + step, NX)
        return other, (pb, other)

    barrier = pltpu.get_barrier_semaphore()
    peers = [z_peer(step) for step in Z_ORDER]
    peers += [slot_peer(step) for step in range(1, NSLOT)]
    peers += [x_peer(step) for step in range(1, NX)]
    for _, device in peers:
        pl.semaphore_signal(barrier, inc=1, device_id=device, device_id_type=MESH)

    chunks = ALONG + ACROSS

    def fetch(chunk):
        first, end = chunks[chunk]
        regions = pl.ds(first, end - first)
        return pltpu.make_async_copy(
            operands[1].at[regions], frames.at[regions], f_sem.at[chunk]
        )

    def bring(i):
        return pltpu.make_async_copy(operands[i], copies[i], in_sem.at[i])

    bring(2).start()
    for chunk in range(len(chunks)):
        fetch(chunk).start()
    others = (0, 3, 4, 5, 6, 7, 8, 9, 10, 11, 12, 13)
    for i in others:
        bring(i).start()

    n = iota((128, 128), 0)
    lane = iota((128, 128), 1)
    zs = hot(lane == ((n & 3) * NZ + (n >> 3)) * NC + ((n >> 2) & 1))
    sz = hot(lane == (((n >> 4) & 3) * NZ + (n & 15)) * NC + (n >> 6))
    bring(2).wait()
    wanted = jnp.broadcast_to(cand_v[pl.ds(slab, 1), :], (512, 128))
    wanted = hot(iota((512, 128), 0) == wanted)

    def z_copy(chunk, step, src, dst, arriving=False):
        first, end = chunks[chunk]
        regions = pl.ds(first, end - first)
        z, device = z_peer(step)
        place = z if arriving else my_z
        return pltpu.make_async_remote_copy(
            src_ref=src.at[z, regions],
            dst_ref=dst.at[place, regions],
            send_sem=a_send.at[chunk, step],
            recv_sem=a_recv.at[chunk, place],
            device_id=device,
            device_id_type=MESH,
        )

    def s_copy(chunk, step, src, dst, arriving=False):
        first, end = chunks[chunk]
        regions = pl.ds(first, end - first)
        slot, device = slot_peer(step)
        place = slot if arriving else my_slot
        return pltpu.make_async_remote_copy(
            src_ref=src.at[slot, regions],
            dst_ref=dst.at[place, regions],
            send_sem=b_send.at[chunk, step],
            recv_sem=b_recv.at[chunk, place],
            device_id=device,
            device_id_type=MESH,
        )

    def x_copy(buffer, send, recv, step, arriving):
        other, device = x_peer(step)
        place = other if arriving else slab
        return pltpu.make_async_remote_copy(
            src_ref=buffer.at[slab],
            dst_ref=buffer.at[place],
            send_sem=send.at[step],
            recv_sem=recv.at[place],
            device_id=device,
            device_id_type=MESH,
        )

    def z_start(chunk, src, dst):
        for step in Z_ORDER:
            z_copy(chunk, step, src, dst).start()
        first, end = chunks[chunk]
        dst[my_z, first:end] = src[my_z, first:end]

    def s_start(chunk, src, dst):
        for step in range(1, NSLOT):
            s_copy(chunk, step, src, dst).start()
        first, end = chunks[chunk]
        dst[my_slot, first:end] = src[my_slot, first:end]

    def z_wait(chunk, src, dst):
        for step in Z_ORDER:
            z_copy(chunk, step, src, dst, True).wait_recv()

    def s_wait(chunk, src, dst):
        for step in range(1, NSLOT):
            s_copy(chunk, step, src, dst, True).wait_recv()

    along = range(len(ALONG))
    across = range(len(ALONG), len(chunks))

    def gather_along(chunk):
        fetch(chunk).wait()
        for s in range(*chunks[chunk]):
            zout[:, s] = dot(by_z, frames[s]).reshape(NZ, NSLOT, 256).astype(BF)

    def gather_across(chunk):
        fetch(chunk).wait()
        for s in range(*chunks[chunk]):
            sout[:, s] = dot(by_slot, frames[s]).reshape(NSLOT, NZ, 256).astype(BF)

    by_z = dot_t(zs, wanted).astype(BF)
    for chunk in along:
        gather_along(chunk)
    by_slot = dot_t(sz, wanted).astype(BF)
    bring(0).wait()
    qi = iota((32, 32), 0)
    pick = hot(iota((32, 32), 1) == 4 * (qi & 7) + (qi >> 3))
    for r in range(9):
        qbuf[slab, r] = dot(pick, q_ref[r]).reshape(4, 8, 256).astype(BF)
    for chunk in across:
        gather_across(chunk)

    pl.semaphore_wait(barrier, len(peers))
    for chunk in along:
        z_start(chunk, zout, zin)
    for chunk in across:
        s_start(chunk, sout, sin)
    for step in range(1, NX):
        x_copy(qbuf, q_send, q_recv, step, False).start()
    for i in others[1:]:
        bring(i).wait()

    to_z = hot(lane == (n & 7) * NZ + (n >> 3))
    to_slot = hot(lane == (2 * (n & 7) + ((n >> 3) & 1)) * NSLOT + (n >> 4))
    place = hot(
        lane == (2 * (n & 7) + (n >> 6)) * NSLOT + ((n >> 5) & 1) * NY + ((n >> 3) & 3)
    )
    for chunk in across:
        s_wait(chunk, sout, sin)
        for s in range(*chunks[chunk]):
            rows = dot(to_z, sin[:, s].reshape(128, 256))
            zmid[:, s] = rows.reshape(NZ, NSLOT, 256).astype(BF)
        z_start(chunk, zmid, xz)

    prepare(k1, b1, k2, b2, k3, b3, k4, sq, w1, w2, w3, b2c, k4c, p1f, p1b, p3h, p3l)

    for chunk in along:
        z_wait(chunk, zout, zin)
        for s in range(*chunks[chunk]):
            rows = dot(to_slot, zin[:, s].reshape(128, 256))
            smid[:, s] = rows.reshape(NSLOT, 2, 8, 256).astype(BF)
        s_start(chunk, smid, xs)
    for step in range(1, NX):
        x_copy(qbuf, q_send, q_recv, step, True).wait_recv()
    for chunk in along:
        s_wait(chunk, smid, xs)
        right = [
            xs[:, s, e].reshape(64, 256) for s in range(*chunks[chunk]) for e in range(2)
        ]
        gram_chunk(chunk, right, qbuf, best)
    for chunk in across:
        z_wait(chunk, zmid, xz)
        right = [
            dot(place, xz[:, s].reshape(128, 256)).astype(BF) for s in range(*chunks[chunk])
        ]
        gram_chunk(chunk, right, qbuf, best)

    qlen = qlen_ref[0]
    clen = clen_ref[cand_s[slab, pb]]
    scores[slab] = refine(
        best, qlen, clen, b4[0], w1, w2, w3, b2c, k4c, p1f, p1b, p2h, p2l, p3h, p3l
    )
    for step in range(1, NX):
        x_copy(scores, s_send, s_recv, step, False).start()
    for chunk in range(len(chunks)):
        line, pair = ((zout, zin), (smid, xs)) if chunk in along else ((zmid, xz), (sout, sin))
        for step in Z_ORDER:
            z_copy(chunk, step, *line).wait_send()
        for step in range(1, NSLOT):
            s_copy(chunk, step, *pair).wait_send()
    for step in range(1, NX):
        x_copy(qbuf, q_send, q_recv, step, False).wait_send()
    for step in range(1, NX):
        x_copy(scores, s_send, s_recv, step, True).wait_recv()
    for step in range(1, NX):
        x_copy(scores, s_send, s_recv, step, False).wait_send()
    where = iota((1, 128), 1)
    line = scores[0, 0:1]
    for other in range(1, NX):
        line = jnp.where(where == other, scores[other, 0:1], line)
    out_ref[...] = line[:, 0:4]


def compute_scratch():
    return [
        pltpu.VMEM((9, 128, 128), F32),
        pltpu.VMEM((128, 128), F32),
        pltpu.VMEM((512, 256), BF),
        pltpu.VMEM((512, 512), BF),
        pltpu.VMEM((256, 640), BF),
        pltpu.VMEM((64, 128), F32),
        pltpu.VMEM((128, 128), F32),
        pltpu.VMEM((384, 128), F32),
        pltpu.VMEM((256, 1024), BF),
        pltpu.VMEM((512, 1024), BF),
        pltpu.VMEM((512, 1024), BF),
        pltpu.VMEM((640, 1024), BF),
        pltpu.VMEM((640, 1024), BF),
    ]


def per_device(
    query_feats, frame_store, candidates, query_length, clip_length,
    kernel_one, bias_one, kernel_two, bias_two, kernel_three, bias_three, kernel_four, bias_four,
):
    vmem = pl.BlockSpec(memory_space=pltpu.VMEM)
    dma = pltpu.SemaphoreType.DMA
    count = len(ALONG + ACROSS)
    pairs = candidates.T
    by_z = pltpu.VMEM((NZ, 9, NSLOT, 256), BF)
    by_slot = pltpu.VMEM((NSLOT, 9, NZ, 256), BF)
    to_gram = pltpu.VMEM((NSLOT, 9, 2, 8, 256), BF)
    return pl.pallas_call(
        kernel,
        out_shape=jax.ShapeDtypeStruct((1, 4), F32),
        in_specs=[pl.BlockSpec(memory_space=pl.ANY)] * 14,
        out_specs=vmem,
        scratch_shapes=[
            pltpu.VMEM((9, 32, 256), BF),
            pltpu.VMEM((9, 512, 256), BF),
            pltpu.VMEM((4, 128), jnp.int32),
            pltpu.SMEM((4, 128), jnp.int32),
            pltpu.SMEM((1,), jnp.int32),
            pltpu.SMEM((512,), jnp.int32),
            pltpu.VMEM((9, 1, 32), F32),
            pltpu.VMEM((1, 32), F32),
            pltpu.VMEM((288, 64), F32),
            pltpu.VMEM((1, 64), F32),
            pltpu.VMEM((576, 128), F32),
            pltpu.VMEM((1, 128), F32),
            pltpu.VMEM((1, 128), F32),
            pltpu.SMEM((1,), F32),
            by_z, by_z, to_gram, to_gram, by_slot, by_slot, by_z, by_z,
            pltpu.VMEM((NX, 9, 4, 8, 256), BF),
        ]
        + compute_scratch()
        + [
            pltpu.VMEM((NX, 8, 128), F32),
            dma((14,)),
            dma((count,)),
            dma((count, NZ)),
            dma((count, NZ)),
            dma((count, NSLOT)),
            dma((count, NSLOT)),
            dma((NX,)),
            dma((NX,)),
            dma((NX,)),
            dma((NX,)),
        ],
        compiler_params=pltpu.CompilerParams(collective_id=0, has_side_effects=True),
        name="score_pairs",
    )(
        query_feats[0].transpose(1, 0, 2),
        frame_store[:, 0].transpose(1, 0, 2),
        pairs,
        pairs,
        query_length,
        clip_length,
        kernel_one.reshape(9, 1, 32),
        bias_one.reshape(1, 32),
        kernel_two.reshape(288, 64),
        bias_two.reshape(1, 64),
        kernel_three.reshape(576, 128),
        bias_three.reshape(1, 128),
        kernel_four.reshape(1, 128),
        bias_four,
    )


def solution(mesh):
    placed = (
        P("pb", "slab", None, None),
        P(None, "pb", None, None),
        P(), P("pb"), P(), P(), P(), P(), P(), P(), P(), P(), P(),
    )
    return jax.shard_map(
        per_device, mesh=mesh, in_specs=placed, out_specs=P("pb", None), check_vma=False
    )
```

```python
import functools

import jax
import jax.numpy as jnp
from jax import lax
from jax.experimental import pallas as pl
from jax.experimental.pallas import tpu as pltpu
from jax.sharding import PartitionSpec as P

NY, NZ, NC, NX = 4, 16, 2, 4
NSLOT = NY * NC
ALONG = ((0, 5),)
ACROSS = ((5, 9),)
MESH = pl.DeviceIdType.MESH
BF = jnp.bfloat16
F32 = jnp.float32
Z_ORDER = (8, 7, 9, 6, 10, 5, 11, 4, 12, 3, 13, 2, 14, 1, 15)


def iota(shape, dim):
    return lax.broadcasted_iota(jnp.int32, shape, dim)


def dot(a, b):
    return lax.dot_general(a, b, (((1,), (0,)), ((), ())), preferred_element_type=F32)


def dot_t(a, b):
    return lax.dot_general(a, b, (((1,), (1,)), ((), ())), preferred_element_type=F32)


def hot(mask):
    return jnp.where(mask, 1.0, 0.0).astype(BF)


def halves(x):
    hi = x.astype(BF)
    lo = (x - hi.astype(F32)).astype(BF)
    return hi, lo


def prepare(k1, b1, k2, b2, k3, b3, k4, sq, w1, w2, w3, b2c, k4c, p1f, p1b):
    sq[...] = jnp.zeros_like(sq)
    for tap in range(9):
        sq[tap : tap + 1, 0:32] = k1[tap]
    sq[9:10, 0:32] = b1[...]
    hi, lo = halves(jnp.transpose(sq[...])[0:32])
    t = iota((128, 256), 0)
    k = iota((128, 256), 1)
    ti = jnp.where(t >= 3, 1, 0) + jnp.where(t >= 6, 1, 0)
    tj = t - 3 * ti
    for phase in range(16):
        row = 2 * (phase >> 3) + ((phase >> 1) & 1)
        col = 2 * ((phase >> 2) & 1) + (phase & 1)
        at = jnp.where(t == 9, 36, (row + ti) * 6 + col + tj)
        at = jnp.where(t > 9, -1000, at)
        both = hot((k == at) | (k == at + 48))
        last = hot(k == at + 96)
        w1[phase * 32 : phase * 32 + 32, :] = (dot(hi, both) + dot(lo, last)).astype(BF)
    w2[...] = jnp.zeros_like(w2)
    for ti in range(3):
        sq[...] = jnp.zeros_like(sq)
        sq[0:96, 0:64] = k2[ti * 96 : ti * 96 + 96, :]
        block = jnp.transpose(sq[...])[0:64]
        for a in range(2):
            for b in range(2):
                hi, lo = halves(block if b == 0 else pltpu.roll(block, 32, 1))
                lanes = slice((a + ti) * 128, (a + ti) * 128 + 128)
                row = (a * 2 + b) * 64
                w2[row : row + 64, lanes] = hi
                w2[256 + row : 256 + row + 64, lanes] = lo
    sq[...] = jnp.zeros_like(sq)
    sq[:, 0:64] = jnp.broadcast_to(b2[...], (128, 64))
    b2c[...] = jnp.transpose(sq[...])[0:64]
    for part in range(5):
        if part < 4:
            block = k3[part * 128 : part * 128 + 128, :]
        else:
            sq[...] = jnp.zeros_like(sq)
            sq[0:64, :] = k3[512:576, :]
            sq[64:65, :] = b3[...]
            block = sq[...]
        hi, lo = halves(jnp.transpose(block))
        w3[0:128, part * 128 : part * 128 + 128] = hi
        w3[128:256, part * 128 : part * 128 + 128] = lo
    k4c[...] = jnp.transpose(jnp.broadcast_to(k4[...], (128, 128)))
    p1b[144:256, :] = jnp.zeros((112, 1024), BF)
    ones = jnp.where(iota((16, 128), 0) == 4, 1.0, 0.0)
    for u in range(8):
        p1f[u * 48 + 32 : u * 48 + 48, :] = ones


def gram_chunk(chunk, right, qbuf, best):
    right = jnp.concatenate(right, axis=0)
    count = right.shape[0] // 128
    for r in range(9):
        g = dot_t(qbuf[:, r].reshape(128, 256), right)
        m = g[:, 0:128]
        for s in range(1, count):
            m = jnp.maximum(m, g[:, s * 128 : s * 128 + 128])
        best[r] = m if chunk == 0 else jnp.maximum(best[r], m)


def refine(best, qlen, clen, b4, w1, w2, w3, b2c, k4c, p1f, p1b, p2h, p2l, p3h, p3l):
    lane = iota((8, 128), 1)
    sub = iota((8, 128), 0)
    grp = lane >> 5
    col = lane & 31
    total = best[0]
    for r in range(1, 9):
        total = total + best[r]
    total = total * (1.0 / 9.0)
    keep_col = (4 * col + grp) < clen
    sim = []
    for g in range(4):
        line = []
        for sg in range(4):
            at = (g * 4 + sg) * 8
            keep = keep_col & ((32 * g + 4 * sub + sg) < qlen)
            line.append(jnp.where(keep, total[at : at + 8], 0.0))
        sim.append(line)

    def up(x, nrow):
        y = pltpu.roll(x, 1, 0)
        z = jnp.where(grp == 0, 0.0, pltpu.roll(y, 32, 1))
        return jnp.where(sub == 0, z, y)

    def down(x, nrow):
        y = pltpu.roll(x, 7, 0)
        z = jnp.where(grp == 3, 0.0, pltpu.roll(y, 96, 1))
        return jnp.where(sub == 7, z, y)

    base = {}
    for sg in range(4):
        for rho in range(4):
            out = None
            for g in range(4):
                shift = ((g - rho) * 32) % 128
                piece = sim[g][sg] if shift == 0 else pltpu.roll(sim[g][sg], shift, 1)
                out = piece if out is None else jnp.where(grp == g, piece, out)
            base[sg, rho] = out
    rows = {}
    for rho in range(4):
        for sg in range(4):
            rows[sg, rho] = base[sg, rho]
        rows[-1, rho] = up(base[3, rho], 8)
        rows[4, rho] = down(base[0, rho], 8)
    for d in range(-1, 5):
        for e in range(-1, 5):
            if e == -1:
                v = jnp.where(col == 0, 0.0, pltpu.roll(rows[d, 3], 1, 1))
            elif e == 4:
                v = jnp.where(col == 31, 0.0, pltpu.roll(rows[d, 0], 127, 1))
            else:
                v = rows[d, e]
            p1f[pl.ds((d + 1) * 6 + e + 1, 8, stride=48), :] = v
    for u in range(8):
        hi, lo = halves(p1f[u * 48 : u * 48 + 48, :])
        lanes = slice(u * 128, u * 128 + 128)
        p1b[0:48, lanes] = hi
        p1b[48:96, lanes] = lo
        p1b[96:144, lanes] = hi

    def tall(x, n):
        return jnp.broadcast_to(x[0:1], (n, 128))

    grp32, col32 = tall(grp, 32), tall(col, 32)
    grp64, col64 = tall(grp, 64), tall(col, 64)

    def put(high, low, at, n, tile, value):
        hi, lo = halves(value)
        high[at : at + n, tile * 128 : tile * 128 + 128] = hi
        low[at : at + n, tile * 128 : tile * 128 + 128] = lo

    def put_before(high, low, at, n, value, groups):
        put(high, low, at, n, 0, jnp.where(groups == 0, 0.0, pltpu.roll(value, 32, 1)))

    def put_after(high, low, at, n, value, groups):
        put(high, low, at, n, 9, jnp.where(groups == 3, 0.0, pltpu.roll(value, 96, 1)))

    def window(ref, first, end, tile, move):
        at = (tile * 2 + 1 + move) * 128
        return ref[first:end, at : at + 256]

    for tile in range(4):
        o1 = dot(w1[...], p1b[:, tile * 256 : tile * 256 + 256])
        for ab in range(4):
            a, b = ab >> 1, ab & 1
            part = o1[ab * 128 : ab * 128 + 128]
            m = jnp.maximum(
                jnp.maximum(part[0:32], part[32:64]), jnp.maximum(part[64:96], part[96:128])
            )
            m = jnp.maximum(m, 0.0)
            for half in range(2):
                u = tile * 2 + half
                v = m[:, half * 128 : half * 128 + 128]
                if b == 1:
                    moved = jnp.where(col32 == 0, 0.0, pltpu.roll(v, 1, 1))
                    variants = ((2, v), (0, moved))
                else:
                    moved = jnp.where(col32 == 31, 0.0, pltpu.roll(v, 127, 1))
                    variants = ((1, v), (3, moved))
                for e, w in variants:
                    at = (a * 4 + e) * 32
                    put(p2h, p2l, at, 32, u + 1, w)
                    if a == 0 and u == 0:
                        put_after(p2h, p2l, at, 32, w, grp32)
                    if a == 1 and u == 7:
                        put_before(p2h, p2l, at, 32, w, grp32)
    for tile in range(4):
        high, low = (
            jnp.concatenate(
                [
                    window(ref, 128, 256, tile, -1),
                    window(ref, 0, 256, tile, 0),
                    window(ref, 0, 128, tile, 1),
                ],
                axis=0,
            )
            for ref in (p2h, p2l)
        )
        first = dot(w2[...], high)
        o2 = first[0:256] + (first[256:512] + dot(w2[0:256, :], low))
        m = jnp.maximum(
            jnp.maximum(o2[0:64], o2[64:128]), jnp.maximum(o2[128:192], o2[192:256])
        )
        for half in range(2):
            u = tile * 2 + half
            v = jnp.maximum(m[:, half * 128 : half * 128 + 128] + b2c[...], 0.0)
            left = jnp.where(col64 == 0, 0.0, pltpu.roll(v, 1, 1))
            right = jnp.where(col64 == 31, 0.0, pltpu.roll(v, 127, 1))
            for dj, w in ((0, left), (1, v), (2, right)):
                put(p3h, p3l, dj * 64, 64, u + 1, w)
                if u == 0:
                    put_after(p3h, p3l, dj * 64, 64, w, grp64)
                if u == 7:
                    put_before(p3h, p3l, dj * 64, 64, w, grp64)
    final = []
    one = hot(iota((64, 256), 0) == 0)
    for tile in range(4):
        high, low = (
            jnp.concatenate(
                [window(ref, 0, 192, tile, move) for move in (-1, 0, 1)] + last, axis=0
            )
            for ref, last in ((p3h, [one]), (p3l, [jnp.zeros_like(one)]))
        )
        first = dot(w3[...], high)
        o3 = first[0:128] + (first[128:256] + dot(w3[0:128, :], low))
        o3 = jnp.maximum(o3, 0.0)
        for half in range(2):
            v = o3[:, half * 128 : half * 128 + 128] * k4c[...]
            final.append(jnp.sum(v, axis=0, keepdims=True))
    field = jnp.clip(jnp.concatenate(final, axis=0) + b4, -1.0, 1.0)
    m = jnp.where(4 * col < clen, field, -2.0)
    for step in (1, 2, 4, 8, 16):
        m = jnp.maximum(m, pltpu.roll(m, 128 - step, 1))
    counted = (col == 0) & (4 * (grp * 8 + sub) < qlen)
    score = jnp.sum(jnp.where(counted, m, 0.0), keepdims=True)
    number = ((jnp.full((8, 128), qlen, jnp.int32) + 3) >> 2).astype(F32)
    return jnp.broadcast_to(score, (8, 128)) / number


def kernel(*refs):
    operands, refs = refs[:14], refs[14:]
    out_ref, refs = refs[0], refs[1:]
    copies, refs = refs[:14], refs[14:]
    (
        zout, zin, smid, xs, sout, sin, zmid, xz, qbuf, best, sq, w1, w2, w3, b2c, k4c,
        p1f, p1b, p2h, p2l, p3h, p3l, scores,
        in_sem, f_sem, a_send, a_recv, b_send, b_recv, q_send, q_recv, s_send, s_recv,
    ) = refs
    q_ref, frames, cand_v, cand_s, qlen_ref, clen_ref, k1, b1, k2, b2, k3, b3, k4, b4 = copies
    pb = lax.axis_index("pb")
    slab = lax.axis_index("slab")
    my_y = lax.div(pb, NZ * NC)
    my_z = lax.rem(lax.div(pb, NC), NZ)
    my_c = lax.rem(pb, NC)
    my_slot = my_c * NY + my_y

    def z_peer(step):
        z = lax.rem(my_z + step, NZ)
        return z, ((my_y * NZ + z) * NC + my_c, slab)

    def slot_peer(step):
        slot = lax.rem(my_slot + step, NSLOT)
        y, c = lax.rem(slot, NY), lax.div(slot, NY)
        return slot, ((y * NZ + my_z) * NC + c, slab)

    def x_peer(step):
        other = lax.rem(slab + step, NX)
        return other, (pb, other)

    barrier = pltpu.get_barrier_semaphore()
    peers = [z_peer(step) for step in Z_ORDER]
    peers += [slot_peer(step) for step in range(1, NSLOT)]
    peers += [x_peer(step) for step in range(1, NX)]
    for _, device in peers:
        pl.semaphore_signal(barrier, inc=1, device_id=device, device_id_type=MESH)

    chunks = ALONG + ACROSS

    def fetch(chunk):
        first, end = chunks[chunk]
        regions = pl.ds(first, end - first)
        return pltpu.make_async_copy(
            operands[1].at[regions], frames.at[regions], f_sem.at[chunk]
        )

    def bring(i):
        return pltpu.make_async_copy(operands[i], copies[i], in_sem.at[i])

    bring(2).start()
    for chunk in range(len(chunks)):
        fetch(chunk).start()
    others = (0, 3, 4, 5, 6, 7, 8, 9, 10, 11, 12, 13)
    for i in others:
        bring(i).start()

    n = iota((128, 128), 0)
    lane = iota((128, 128), 1)
    zs = hot(lane == ((n & 3) * NZ + (n >> 3)) * NC + ((n >> 2) & 1))
    sz = hot(lane == (((n >> 4) & 3) * NZ + (n & 15)) * NC + (n >> 6))
    bring(2).wait()
    wanted = jnp.broadcast_to(cand_v[pl.ds(slab, 1), :], (512, 128))
    wanted = hot(iota((512, 128), 0) == wanted)

    def z_copy(chunk, step, src, dst):
        first, end = chunks[chunk]
        regions = pl.ds(first, end - first)
        z, device = z_peer(step)
        return pltpu.make_async_remote_copy(
            src_ref=src.at[z, regions],
            dst_ref=dst.at[my_z, regions],
            send_sem=a_send.at[chunk],
            recv_sem=a_recv.at[chunk],
            device_id=device,
            device_id_type=MESH,
        )

    def s_copy(chunk, step, src, dst):
        first, end = chunks[chunk]
        regions = pl.ds(first, end - first)
        slot, device = slot_peer(step)
        return pltpu.make_async_remote_copy(
            src_ref=src.at[slot, regions],
            dst_ref=dst.at[my_slot, regions],
            send_sem=b_send.at[chunk],
            recv_sem=b_recv.at[chunk],
            device_id=device,
            device_id_type=MESH,
        )

    def x_copy(buffer, send, recv, step):
        other, device = x_peer(step)
        return pltpu.make_async_remote_copy(
            src_ref=buffer.at[slab],
            dst_ref=buffer.at[slab],
            send_sem=send.at[0],
            recv_sem=recv.at[0],
            device_id=device,
            device_id_type=MESH,
        )

    def z_start(chunk, src, dst):
        for step in Z_ORDER:
            z_copy(chunk, step, src, dst).start()
        first, end = chunks[chunk]
        dst[my_z, first:end] = src[my_z, first:end]

    def s_start(chunk, src, dst):
        for step in range(1, NSLOT):
            s_copy(chunk, step, src, dst).start()
        first, end = chunks[chunk]
        dst[my_slot, first:end] = src[my_slot, first:end]

    def z_group(chunk, src, dst):
        first, end = chunks[chunk]
        return pltpu.make_async_remote_copy(
            src_ref=src.at[pl.ds(0, NZ - 1), pl.ds(first, end - first)],
            dst_ref=dst.at[pl.ds(0, NZ - 1), pl.ds(first, end - first)],
            send_sem=a_send.at[chunk],
            recv_sem=a_recv.at[chunk],
            device_id=z_peer(1)[1],
            device_id_type=MESH,
        )

    def s_group(chunk, src, dst):
        first, end = chunks[chunk]
        return pltpu.make_async_remote_copy(
            src_ref=src.at[pl.ds(0, NSLOT - 1), pl.ds(first, end - first)],
            dst_ref=dst.at[pl.ds(0, NSLOT - 1), pl.ds(first, end - first)],
            send_sem=b_send.at[chunk],
            recv_sem=b_recv.at[chunk],
            device_id=slot_peer(1)[1],
            device_id_type=MESH,
        )

    def x_group(buffer, send, recv):
        return pltpu.make_async_remote_copy(
            src_ref=buffer.at[pl.ds(0, NX - 1)],
            dst_ref=buffer.at[pl.ds(0, NX - 1)],
            send_sem=send.at[0],
            recv_sem=recv.at[0],
            device_id=x_peer(1)[1],
            device_id_type=MESH,
        )

    along = range(len(ALONG))
    across = range(len(ALONG), len(chunks))

    def gather_along(chunk):
        fetch(chunk).wait()
        for s in range(*chunks[chunk]):
            zout[:, s] = dot(by_z, frames[s]).reshape(NZ, NSLOT, 256).astype(BF)

    def gather_across(chunk):
        fetch(chunk).wait()
        for s in range(*chunks[chunk]):
            sout[:, s] = dot(by_slot, frames[s]).reshape(NSLOT, NZ, 256).astype(BF)

    by_z = dot_t(zs, wanted).astype(BF)
    for chunk in along:
        gather_along(chunk)
    by_slot = dot_t(sz, wanted).astype(BF)
    bring(0).wait()
    qi = iota((32, 32), 0)
    pick = hot(iota((32, 32), 1) == 4 * (qi & 7) + (qi >> 3))
    for r in range(9):
        qbuf[slab, r] = dot(pick, q_ref[r]).reshape(4, 8, 256).astype(BF)
    for chunk in across:
        gather_across(chunk)

    pl.semaphore_wait(barrier, len(peers))
    for chunk in along:
        z_start(chunk, zout, zin)
    for chunk in across:
        s_start(chunk, sout, sin)
    for step in range(1, NX):
        x_copy(qbuf, q_send, q_recv, step).start()
    for i in others[1:]:
        bring(i).wait()

    to_z = hot(lane == (n & 7) * NZ + (n >> 3))
    to_slot = hot(lane == (2 * (n & 7) + ((n >> 3) & 1)) * NSLOT + (n >> 4))
    place = hot(
        lane == (2 * (n & 7) + (n >> 6)) * NSLOT + ((n >> 5) & 1) * NY + ((n >> 3) & 3)
    )
    for chunk in across:
        s_group(chunk, sout, sin).wait_recv()
        for s in range(*chunks[chunk]):
            rows = dot(to_z, sin[:, s].reshape(128, 256))
            zmid[:, s] = rows.reshape(NZ, NSLOT, 256).astype(BF)
        z_start(chunk, zmid, xz)

    prepare(k1, b1, k2, b2, k3, b3, k4, sq, w1, w2, w3, b2c, k4c, p1f, p1b)

    for chunk in along:
        z_group(chunk, zout, zin).wait_recv()
        for s in range(*chunks[chunk]):
            rows = dot(to_slot, zin[:, s].reshape(128, 256))
            smid[:, s] = rows.reshape(NSLOT, 2, 8, 256).astype(BF)
        s_start(chunk, smid, xs)
    x_group(qbuf, q_send, q_recv).wait_recv()
    for chunk in along:
        s_group(chunk, smid, xs).wait_recv()
        right = [
            xs[:, s, e].reshape(64, 256) for s in range(*chunks[chunk]) for e in range(2)
        ]
        gram_chunk(chunk, right, qbuf, best)
    for chunk in across:
        z_group(chunk, zmid, xz).wait_recv()
        right = [
            dot(place, xz[:, s].reshape(128, 256)).astype(BF) for s in range(*chunks[chunk])
        ]
        gram_chunk(chunk, right, qbuf, best)

    qlen = qlen_ref[0]
    clen = clen_ref[cand_s[slab, pb]]
    scores[slab] = refine(
        best, qlen, clen, b4[0], w1, w2, w3, b2c, k4c, p1f, p1b, p2h, p2l, p3h, p3l
    )
    for step in range(1, NX):
        x_copy(scores, s_send, s_recv, step).start()
    for chunk in range(len(chunks)):
        line, pair = ((zout, zin), (smid, xs)) if chunk in along else ((zmid, xz), (sout, sin))
        z_group(chunk, *line).wait_send()
        s_group(chunk, *pair).wait_send()
    x_group(qbuf, q_send, q_recv).wait_send()
    x_group(scores, s_send, s_recv).wait_send()
    x_group(scores, s_send, s_recv).wait_recv()
    where = iota((1, 128), 1)
    line = scores[0, 0:1]
    for other in range(1, NX):
        line = jnp.where(where == other, scores[other, 0:1], line)
    out_ref[...] = line[:, 0:4]


def compute_scratch():
    return [
        pltpu.VMEM((9, 128, 128), F32),
        pltpu.VMEM((128, 128), F32),
        pltpu.VMEM((512, 256), BF),
        pltpu.VMEM((512, 512), BF),
        pltpu.VMEM((256, 640), BF),
        pltpu.VMEM((64, 128), F32),
        pltpu.VMEM((128, 128), F32),
        pltpu.VMEM((384, 128), F32),
        pltpu.VMEM((256, 1024), BF),
        pltpu.VMEM((256, 1280), BF),
        pltpu.VMEM((256, 1280), BF),
        pltpu.VMEM((192, 1280), BF),
        pltpu.VMEM((192, 1280), BF),
    ]


def per_device(
    query_feats, frame_store, candidates, query_length, clip_length,
    kernel_one, bias_one, kernel_two, bias_two, kernel_three, bias_three, kernel_four, bias_four,
):
    vmem = pl.BlockSpec(memory_space=pltpu.VMEM)
    dma = pltpu.SemaphoreType.DMA
    count = len(ALONG + ACROSS)
    pairs = candidates.T
    by_z = pltpu.VMEM((NZ, 9, NSLOT, 256), BF)
    by_slot = pltpu.VMEM((NSLOT, 9, NZ, 256), BF)
    to_gram = pltpu.VMEM((NSLOT, 9, 2, 8, 256), BF)
    return pl.pallas_call(
        kernel,
        out_shape=jax.ShapeDtypeStruct((1, 4), F32),
        in_specs=[pl.BlockSpec(memory_space=pl.ANY)] * 14,
        out_specs=vmem,
        scratch_shapes=[
            pltpu.VMEM((9, 32, 256), BF),
            pltpu.VMEM((9, 512, 256), BF),
            pltpu.VMEM((4, 128), jnp.int32),
            pltpu.SMEM((4, 128), jnp.int32),
            pltpu.SMEM((1,), jnp.int32),
            pltpu.SMEM((512,), jnp.int32),
            pltpu.VMEM((9, 1, 32), F32),
            pltpu.VMEM((1, 32), F32),
            pltpu.VMEM((288, 64), F32),
            pltpu.VMEM((1, 64), F32),
            pltpu.VMEM((576, 128), F32),
            pltpu.VMEM((1, 128), F32),
            pltpu.VMEM((1, 128), F32),
            pltpu.SMEM((1,), F32),
            by_z, by_z, to_gram, to_gram, by_slot, by_slot, by_z, by_z,
            pltpu.VMEM((NX, 9, 4, 8, 256), BF),
        ]
        + compute_scratch()
        + [
            pltpu.VMEM((NX, 8, 128), F32),
            dma((14,)),
            dma((count,)),
            dma((count,)),
            dma((count,)),
            dma((count,)),
            dma((count,)),
            dma((1,)),
            dma((1,)),
            dma((1,)),
            dma((1,)),
        ],
        compiler_params=pltpu.CompilerParams(collective_id=0, has_side_effects=True),
        name="score_pairs",
    )(
        query_feats[0].transpose(1, 0, 2),
        frame_store[:, 0].transpose(1, 0, 2),
        pairs,
        pairs,
        query_length,
        clip_length,
        kernel_one.reshape(9, 1, 32),
        bias_one.reshape(1, 32),
        kernel_two.reshape(288, 64),
        bias_two.reshape(1, 64),
        kernel_three.reshape(576, 128),
        bias_three.reshape(1, 128),
        kernel_four.reshape(1, 128),
        bias_four,
    )


def solution(mesh):
    placed = (
        P("pb", "slab", None, None),
        P(None, "pb", None, None),
        P(), P("pb"), P(), P(), P(), P(), P(), P(), P(), P(), P(),
    )
    return jax.shard_map(
        per_device, mesh=mesh, in_specs=placed, out_specs=P("pb", None), check_vma=False
    )
```

```python
import functools

import jax
import jax.numpy as jnp
from jax import lax
from jax.experimental import pallas as pl
from jax.experimental.pallas import tpu as pltpu
from jax.sharding import PartitionSpec as P

NY, NZ, NC, NX = 4, 16, 2, 4
NSLOT = NY * NC
ALONG = ((0, 5),)
ACROSS = ((5, 9),)
MESH = pl.DeviceIdType.MESH
BF = jnp.bfloat16
F32 = jnp.float32
Z_ORDER = (8, 7, 9, 6, 10, 5, 11, 4, 12, 3, 13, 2, 14, 1, 15)


def iota(shape, dim):
    return lax.broadcasted_iota(jnp.int32, shape, dim)


def dot(a, b):
    return lax.dot_general(a, b, (((1,), (0,)), ((), ())), preferred_element_type=F32)


def dot_t(a, b):
    return lax.dot_general(a, b, (((1,), (1,)), ((), ())), preferred_element_type=F32)


def hot(mask):
    return jnp.where(mask, 1.0, 0.0).astype(BF)


def halves(x):
    hi = x.astype(BF)
    lo = (x - hi.astype(F32)).astype(BF)
    return hi, lo


def prepare(k1, b1, k2, b2, k3, b3, k4, sq, w1, w2, w3, b2c, k4c, p1f, p1b):
    sq[...] = jnp.zeros_like(sq)
    for tap in range(9):
        sq[tap : tap + 1, 0:32] = k1[tap]
    sq[9:10, 0:32] = b1[...]
    hi, lo = halves(jnp.transpose(sq[...])[0:32])
    t = iota((128, 256), 0)
    k = iota((128, 256), 1)
    ti = jnp.where(t >= 3, 1, 0) + jnp.where(t >= 6, 1, 0)
    tj = t - 3 * ti
    for phase in range(16):
        row = 2 * (phase >> 3) + ((phase >> 1) & 1)
        col = 2 * ((phase >> 2) & 1) + (phase & 1)
        at = jnp.where(t == 9, 36, (row + ti) * 6 + col + tj)
        at = jnp.where(t > 9, -1000, at)
        both = hot((k == at) | (k == at + 48))
        last = hot(k == at + 96)
        w1[phase * 32 : phase * 32 + 32, :] = (dot(hi, both) + dot(lo, last)).astype(BF)
    w2[...] = jnp.zeros_like(w2)
    for ti in range(3):
        sq[...] = jnp.zeros_like(sq)
        sq[0:96, 0:64] = k2[ti * 96 : ti * 96 + 96, :]
        block = jnp.transpose(sq[...])[0:64]
        for a in range(2):
            for b in range(2):
                hi, lo = halves(block if b == 0 else pltpu.roll(block, 32, 1))
                lanes = slice((a + ti) * 128, (a + ti) * 128 + 128)
                row = (a * 2 + b) * 64
                w2[row : row + 64, lanes] = hi
                w2[256 + row : 256 + row + 64, lanes] = lo
    sq[...] = jnp.zeros_like(sq)
    sq[:, 0:64] = jnp.broadcast_to(b2[...], (128, 64))
    b2c[...] = jnp.transpose(sq[...])[0:64]
    for part in range(5):
        if part < 4:
            block = k3[part * 128 : part * 128 + 128, :]
        else:
            sq[...] = jnp.zeros_like(sq)
            sq[0:64, :] = k3[512:576, :]
            sq[64:65, :] = b3[...]
            block = sq[...]
        hi, lo = halves(jnp.transpose(block))
        w3[0:128, part * 128 : part * 128 + 128] = hi
        w3[128:256, part * 128 : part * 128 + 128] = lo
    k4c[...] = jnp.transpose(jnp.broadcast_to(k4[...], (128, 128)))
    p1b[144:256, :] = jnp.zeros((112, 1024), BF)
    ones = jnp.where(iota((16, 128), 0) == 4, 1.0, 0.0)
    for u in range(8):
        p1f[u * 48 + 32 : u * 48 + 48, :] = ones


def gram_chunk(chunk, right, qbuf, best):
    right = jnp.concatenate(right, axis=0)
    count = right.shape[0] // 128
    for r in range(9):
        g = dot_t(qbuf[:, r].reshape(128, 256), right)
        m = g[:, 0:128]
        for s in range(1, count):
            m = jnp.maximum(m, g[:, s * 128 : s * 128 + 128])
        best[r] = m if chunk == 0 else jnp.maximum(best[r], m)


def refine(best, qlen, clen, b4, w1, w2, w3, b2c, k4c, p1f, p1b, p2h, p2l, p3h, p3l):
    lane = iota((8, 128), 1)
    sub = iota((8, 128), 0)
    grp = lane >> 5
    col = lane & 31
    total = best[0]
    for r in range(1, 9):
        total = total + best[r]
    total = total * (1.0 / 9.0)
    keep_col = (4 * col + grp) < clen
    sim = []
    for g in range(4):
        line = []
        for sg in range(4):
            at = (g * 4 + sg) * 8
            keep = keep_col & ((32 * g + 4 * sub + sg) < qlen)
            line.append(jnp.where(keep, total[at : at + 8], 0.0))
        sim.append(line)

    def up(x, nrow):
        y = pltpu.roll(x, 1, 0)
        z = jnp.where(grp == 0, 0.0, pltpu.roll(y, 32, 1))
        return jnp.where(sub == 0, z, y)

    def down(x, nrow):
        y = pltpu.roll(x, 7, 0)
        z = jnp.where(grp == 3, 0.0, pltpu.roll(y, 96, 1))
        return jnp.where(sub == 7, z, y)

    base = {}
    for sg in range(4):
        for rho in range(4):
            out = None
            for g in range(4):
                shift = ((g - rho) * 32) % 128
                piece = sim[g][sg] if shift == 0 else pltpu.roll(sim[g][sg], shift, 1)
                out = piece if out is None else jnp.where(grp == g, piece, out)
            base[sg, rho] = out
    rows = {}
    for rho in range(4):
        for sg in range(4):
            rows[sg, rho] = base[sg, rho]
        rows[-1, rho] = up(base[3, rho], 8)
        rows[4, rho] = down(base[0, rho], 8)
    for d in range(-1, 5):
        for e in range(-1, 5):
            if e == -1:
                v = jnp.where(col == 0, 0.0, pltpu.roll(rows[d, 3], 1, 1))
            elif e == 4:
                v = jnp.where(col == 31, 0.0, pltpu.roll(rows[d, 0], 127, 1))
            else:
                v = rows[d, e]
            p1f[pl.ds((d + 1) * 6 + e + 1, 8, stride=48), :] = v
    for u in range(8):
        hi, lo = halves(p1f[u * 48 : u * 48 + 48, :])
        lanes = slice(u * 128, u * 128 + 128)
        p1b[0:48, lanes] = hi
        p1b[48:96, lanes] = lo
        p1b[96:144, lanes] = hi

    def tall(x, n):
        return jnp.broadcast_to(x[0:1], (n, 128))

    grp32, col32 = tall(grp, 32), tall(col, 32)
    grp64, col64 = tall(grp, 64), tall(col, 64)

    def put(high, low, at, n, tile, value):
        hi, lo = halves(value)
        high[at : at + n, tile * 128 : tile * 128 + 128] = hi
        low[at : at + n, tile * 128 : tile * 128 + 128] = lo

    def put_before(high, low, at, n, value, groups):
        put(high, low, at, n, 0, jnp.where(groups == 0, 0.0, pltpu.roll(value, 32, 1)))

    def put_after(high, low, at, n, value, groups):
        put(high, low, at, n, 9, jnp.where(groups == 3, 0.0, pltpu.roll(value, 96, 1)))

    def window(ref, first, end, tile, move):
        at = (tile * 2 + 1 + move) * 128
        return ref[first:end, at : at + 256]

    for tile in range(4):
        o1 = dot(w1[...], p1b[:, tile * 256 : tile * 256 + 256])
        for ab in range(4):
            a, b = ab >> 1, ab & 1
            part = o1[ab * 128 : ab * 128 + 128]
            m = jnp.maximum(
                jnp.maximum(part[0:32], part[32:64]), jnp.maximum(part[64:96], part[96:128])
            )
            m = jnp.maximum(m, 0.0)
            for half in range(2):
                u = tile * 2 + half
                v = m[:, half * 128 : half * 128 + 128]
                if b == 1:
                    moved = jnp.where(col32 == 0, 0.0, pltpu.roll(v, 1, 1))
                    variants = ((2, v), (0, moved))
                else:
                    moved = jnp.where(col32 == 31, 0.0, pltpu.roll(v, 127, 1))
                    variants = ((1, v), (3, moved))
                for e, w in variants:
                    at = (a * 4 + e) * 32
                    put(p2h, p2l, at, 32, u + 1, w)
                    if a == 0 and u == 0:
                        put_after(p2h, p2l, at, 32, w, grp32)
                    if a == 1 and u == 7:
                        put_before(p2h, p2l, at, 32, w, grp32)
    for tile in range(4):
        high, low = (
            jnp.concatenate(
                [
                    window(ref, 128, 256, tile, -1),
                    window(ref, 0, 256, tile, 0),
                    window(ref, 0, 128, tile, 1),
                ],
                axis=0,
            )
            for ref in (p2h, p2l)
        )
        first = dot(w2[...], high)
        o2 = first[0:256] + (first[256:512] + dot(w2[0:256, :], low))
        m = jnp.maximum(
            jnp.maximum(o2[0:64], o2[64:128]), jnp.maximum(o2[128:192], o2[192:256])
        )
        for half in range(2):
            u = tile * 2 + half
            v = jnp.maximum(m[:, half * 128 : half * 128 + 128] + b2c[...], 0.0)
            left = jnp.where(col64 == 0, 0.0, pltpu.roll(v, 1, 1))
            right = jnp.where(col64 == 31, 0.0, pltpu.roll(v, 127, 1))
            for dj, w in ((0, left), (1, v), (2, right)):
                put(p3h, p3l, dj * 64, 64, u + 1, w)
                if u == 0:
                    put_after(p3h, p3l, dj * 64, 64, w, grp64)
                if u == 7:
                    put_before(p3h, p3l, dj * 64, 64, w, grp64)
    final = []
    one = hot(iota((64, 256), 0) == 0)
    for tile in range(4):
        high, low = (
            jnp.concatenate(
                [window(ref, 0, 192, tile, move) for move in (-1, 0, 1)] + last, axis=0
            )
            for ref, last in ((p3h, [one]), (p3l, [jnp.zeros_like(one)]))
        )
        first = dot(w3[...], high)
        o3 = first[0:128] + (first[128:256] + dot(w3[0:128, :], low))
        o3 = jnp.maximum(o3, 0.0)
        for half in range(2):
            v = o3[:, half * 128 : half * 128 + 128] * k4c[...]
            final.append(jnp.sum(v, axis=0, keepdims=True))
    field = jnp.clip(jnp.concatenate(final, axis=0) + b4, -1.0, 1.0)
    m = jnp.where(4 * col < clen, field, -2.0)
    for step in (1, 2, 4, 8, 16):
        m = jnp.maximum(m, pltpu.roll(m, 128 - step, 1))
    counted = (col == 0) & (4 * (grp * 8 + sub) < qlen)
    score = jnp.sum(jnp.where(counted, m, 0.0), keepdims=True)
    number = ((jnp.full((8, 128), qlen, jnp.int32) + 3) >> 2).astype(F32)
    return jnp.broadcast_to(score, (8, 128)) / number


def kernel(*refs):
    operands, refs = refs[:14], refs[14:]
    out_ref, refs = refs[0], refs[1:]
    copies, refs = refs[:14], refs[14:]
    (
        zout, zin, smid, xs, sout, sin, zmid, xz, qbuf, best, sq, w1, w2, w3, b2c, k4c,
        p1f, p1b, p2h, p2l, p3h, p3l, scores,
        in_sem, f_sem, a_send, a_recv, b_send, b_recv, q_send, q_recv, s_send, s_recv,
    ) = refs
    q_ref, frames, cand_v, cand_s, qlen_ref, clen_ref, k1, b1, k2, b2, k3, b3, k4, b4 = copies
    pb = lax.axis_index("pb")
    slab = lax.axis_index("slab")
    my_y = lax.div(pb, NZ * NC)
    my_z = lax.rem(lax.div(pb, NC), NZ)
    my_c = lax.rem(pb, NC)
    my_slot = my_c * NY + my_y

    def z_peer(step):
        z = lax.rem(my_z + step, NZ)
        return z, ((my_y * NZ + z) * NC + my_c, slab)

    def slot_peer(step):
        slot = lax.rem(my_slot + step, NSLOT)
        y, c = lax.rem(slot, NY), lax.div(slot, NY)
        return slot, ((y * NZ + my_z) * NC + c, slab)

    def x_peer(step):
        other = lax.rem(slab + step, NX)
        return other, (pb, other)

    barrier = pltpu.get_barrier_semaphore()
    peers = [z_peer(step) for step in Z_ORDER]
    peers += [slot_peer(step) for step in range(1, NSLOT)]
    peers += [x_peer(step) for step in range(1, NX)]
    for _, device in peers:
        pl.semaphore_signal(barrier, inc=1, device_id=device, device_id_type=MESH)

    chunks = ALONG + ACROSS

    def fetch(chunk):
        first, end = chunks[chunk]
        regions = pl.ds(first, end - first)
        return pltpu.make_async_copy(
            operands[1].at[regions], frames.at[regions], f_sem.at[chunk]
        )

    def bring(i):
        return pltpu.make_async_copy(operands[i], copies[i], in_sem.at[i])

    bring(2).start()
    for chunk in range(len(chunks)):
        fetch(chunk).start()
    others = (0, 3, 4, 5, 6, 7, 8, 9, 10, 11, 12, 13)
    for i in others:
        bring(i).start()

    n = iota((128, 128), 0)
    lane = iota((128, 128), 1)
    zs = hot(lane == ((n & 3) * NZ + (n >> 3)) * NC + ((n >> 2) & 1))
    sz = hot(lane == (((n >> 4) & 3) * NZ + (n & 15)) * NC + (n >> 6))
    bring(2).wait()
    wanted = jnp.broadcast_to(cand_v[pl.ds(slab, 1), :], (512, 128))
    wanted = hot(iota((512, 128), 0) == wanted)

    def z_copy(chunk, step, src, dst):
        first, end = chunks[chunk]
        regions = pl.ds(first, end - first)
        z, device = z_peer(step)
        return pltpu.make_async_remote_copy(
            src_ref=src.at[z, regions],
            dst_ref=dst.at[my_z, regions],
            send_sem=a_send.at[chunk],
            recv_sem=a_recv.at[chunk],
            device_id=device,
            device_id_type=MESH,
        )

    def s_copy(chunk, step, src, dst):
        first, end = chunks[chunk]
        regions = pl.ds(first, end - first)
        slot, device = slot_peer(step)
        return pltpu.make_async_remote_copy(
            src_ref=src.at[slot, regions],
            dst_ref=dst.at[my_slot, regions],
            send_sem=b_send.at[chunk],
            recv_sem=b_recv.at[chunk],
            device_id=device,
            device_id_type=MESH,
        )

    def x_copy(buffer, send, recv, step):
        other, device = x_peer(step)
        return pltpu.make_async_remote_copy(
            src_ref=buffer.at[slab],
            dst_ref=buffer.at[slab],
            send_sem=send.at[0],
            recv_sem=recv.at[0],
            device_id=device,
            device_id_type=MESH,
        )

    def z_start(chunk, src, dst):
        for step in Z_ORDER:
            z_copy(chunk, step, src, dst).start()
        first, end = chunks[chunk]
        dst[my_z, first:end] = src[my_z, first:end]

    def s_start(chunk, src, dst):
        for step in range(1, NSLOT):
            s_copy(chunk, step, src, dst).start()
        first, end = chunks[chunk]
        dst[my_slot, first:end] = src[my_slot, first:end]

    def z_group(chunk, src, dst):
        first, end = chunks[chunk]
        return pltpu.make_async_remote_copy(
            src_ref=src.at[pl.ds(0, NZ - 1), pl.ds(first, end - first)],
            dst_ref=dst.at[pl.ds(0, NZ - 1), pl.ds(first, end - first)],
            send_sem=a_send.at[chunk],
            recv_sem=a_recv.at[chunk],
            device_id=z_peer(1)[1],
            device_id_type=MESH,
        )

    def s_group(chunk, src, dst):
        first, end = chunks[chunk]
        return pltpu.make_async_remote_copy(
            src_ref=src.at[pl.ds(0, NSLOT - 1), pl.ds(first, end - first)],
            dst_ref=dst.at[pl.ds(0, NSLOT - 1), pl.ds(first, end - first)],
            send_sem=b_send.at[chunk],
            recv_sem=b_recv.at[chunk],
            device_id=slot_peer(1)[1],
            device_id_type=MESH,
        )

    def x_group(buffer, send, recv):
        return pltpu.make_async_remote_copy(
            src_ref=buffer.at[pl.ds(0, NX - 1)],
            dst_ref=buffer.at[pl.ds(0, NX - 1)],
            send_sem=send.at[0],
            recv_sem=recv.at[0],
            device_id=x_peer(1)[1],
            device_id_type=MESH,
        )

    along = range(len(ALONG))
    across = range(len(ALONG), len(chunks))

    def gather_along(chunk):
        fetch(chunk).wait()
        for s in range(*chunks[chunk]):
            zout[:, s] = dot(by_z, frames[s]).reshape(NZ, NSLOT, 256).astype(BF)

    def gather_across(chunk):
        fetch(chunk).wait()
        for s in range(*chunks[chunk]):
            sout[:, s] = dot(by_slot, frames[s]).reshape(NSLOT, NZ, 256).astype(BF)

    by_z = dot_t(zs, wanted).astype(BF)
    for chunk in along:
        gather_along(chunk)
    by_slot = dot_t(sz, wanted).astype(BF)
    bring(0).wait()
    qi = iota((32, 32), 0)
    pick = hot(iota((32, 32), 1) == 4 * (qi & 7) + (qi >> 3))
    for r in range(9):
        qbuf[slab, r] = dot(pick, q_ref[r]).reshape(4, 8, 256).astype(BF)
    for chunk in across:
        gather_across(chunk)

    pl.semaphore_wait(barrier, len(peers))
    for chunk in across:
        s_start(chunk, sout, sin)
    for chunk in along:
        z_start(chunk, zout, zin)
    for step in range(1, NX):
        x_copy(qbuf, q_send, q_recv, step).start()
    for i in others[1:]:
        bring(i).wait()

    to_z = hot(lane == (n & 7) * NZ + (n >> 3))
    to_slot = hot(lane == (2 * (n & 7) + ((n >> 3) & 1)) * NSLOT + (n >> 4))
    place = hot(
        lane == (2 * (n & 7) + (n >> 6)) * NSLOT + ((n >> 5) & 1) * NY + ((n >> 3) & 3)
    )
    for chunk in across:
        s_group(chunk, sout, sin).wait_recv()
        for s in range(*chunks[chunk]):
            rows = dot(to_z, sin[:, s].reshape(128, 256))
            zmid[:, s] = rows.reshape(NZ, NSLOT, 256).astype(BF)
        z_start(chunk, zmid, xz)

    prepare(k1, b1, k2, b2, k3, b3, k4, sq, w1, w2, w3, b2c, k4c, p1f, p1b)

    for chunk in along:
        z_group(chunk, zout, zin).wait_recv()
        for s in range(*chunks[chunk]):
            rows = dot(to_slot, zin[:, s].reshape(128, 256))
            smid[:, s] = rows.reshape(NSLOT, 2, 8, 256).astype(BF)
        s_start(chunk, smid, xs)
    x_group(qbuf, q_send, q_recv).wait_recv()
    for chunk in along:
        s_group(chunk, smid, xs).wait_recv()
        right = [
            xs[:, s, e].reshape(64, 256) for s in range(*chunks[chunk]) for e in range(2)
        ]
        gram_chunk(chunk, right, qbuf, best)
    for chunk in across:
        z_group(chunk, zmid, xz).wait_recv()
        right = [
            dot(place, xz[:, s].reshape(128, 256)).astype(BF) for s in range(*chunks[chunk])
        ]
        gram_chunk(chunk, right, qbuf, best)

    qlen = qlen_ref[0]
    clen = clen_ref[cand_s[slab, pb]]
    scores[slab] = refine(
        best, qlen, clen, b4[0], w1, w2, w3, b2c, k4c, p1f, p1b, p2h, p2l, p3h, p3l
    )
    for step in range(1, NX):
        x_copy(scores, s_send, s_recv, step).start()
    for chunk in range(len(chunks)):
        line, pair = ((zout, zin), (smid, xs)) if chunk in along else ((zmid, xz), (sout, sin))
        z_group(chunk, *line).wait_send()
        s_group(chunk, *pair).wait_send()
    x_group(qbuf, q_send, q_recv).wait_send()
    x_group(scores, s_send, s_recv).wait_send()
    x_group(scores, s_send, s_recv).wait_recv()
    where = iota((1, 128), 1)
    line = scores[0, 0:1]
    for other in range(1, NX):
        line = jnp.where(where == other, scores[other, 0:1], line)
    out_ref[...] = line[:, 0:4]


def compute_scratch():
    return [
        pltpu.VMEM((9, 128, 128), F32),
        pltpu.VMEM((128, 128), F32),
        pltpu.VMEM((512, 256), BF),
        pltpu.VMEM((512, 512), BF),
        pltpu.VMEM((256, 640), BF),
        pltpu.VMEM((64, 128), F32),
        pltpu.VMEM((128, 128), F32),
        pltpu.VMEM((384, 128), F32),
        pltpu.VMEM((256, 1024), BF),
        pltpu.VMEM((256, 1280), BF),
        pltpu.VMEM((256, 1280), BF),
        pltpu.VMEM((192, 1280), BF),
        pltpu.VMEM((192, 1280), BF),
    ]


def per_device(
    query_feats, frame_store, candidates, query_length, clip_length,
    kernel_one, bias_one, kernel_two, bias_two, kernel_three, bias_three, kernel_four, bias_four,
):
    vmem = pl.BlockSpec(memory_space=pltpu.VMEM)
    dma = pltpu.SemaphoreType.DMA
    count = len(ALONG + ACROSS)
    pairs = candidates.T
    by_z = pltpu.VMEM((NZ, 9, NSLOT, 256), BF)
    by_slot = pltpu.VMEM((NSLOT, 9, NZ, 256), BF)
    to_gram = pltpu.VMEM((NSLOT, 9, 2, 8, 256), BF)
    return pl.pallas_call(
        kernel,
        out_shape=jax.ShapeDtypeStruct((1, 4), F32),
        in_specs=[pl.BlockSpec(memory_space=pl.ANY)] * 14,
        out_specs=vmem,
        scratch_shapes=[
            pltpu.VMEM((9, 32, 256), BF),
            pltpu.VMEM((9, 512, 256), BF),
            pltpu.VMEM((4, 128), jnp.int32),
            pltpu.SMEM((4, 128), jnp.int32),
            pltpu.SMEM((1,), jnp.int32),
            pltpu.SMEM((512,), jnp.int32),
            pltpu.VMEM((9, 1, 32), F32),
            pltpu.VMEM((1, 32), F32),
            pltpu.VMEM((288, 64), F32),
            pltpu.VMEM((1, 64), F32),
            pltpu.VMEM((576, 128), F32),
            pltpu.VMEM((1, 128), F32),
            pltpu.VMEM((1, 128), F32),
            pltpu.SMEM((1,), F32),
            by_z, by_z, to_gram, to_gram, by_slot, by_slot, by_z, by_z,
            pltpu.VMEM((NX, 9, 4, 8, 256), BF),
        ]
        + compute_scratch()
        + [
            pltpu.VMEM((NX, 8, 128), F32),
            dma((14,)),
            dma((count,)),
            dma((count,)),
            dma((count,)),
            dma((count,)),
            dma((count,)),
            dma((1,)),
            dma((1,)),
            dma((1,)),
            dma((1,)),
        ],
        compiler_params=pltpu.CompilerParams(collective_id=0, has_side_effects=True),
        name="score_pairs",
    )(
        query_feats[0].transpose(1, 0, 2),
        frame_store[:, 0].transpose(1, 0, 2),
        pairs,
        pairs,
        query_length,
        clip_length,
        kernel_one.reshape(9, 1, 32),
        bias_one.reshape(1, 32),
        kernel_two.reshape(288, 64),
        bias_two.reshape(1, 64),
        kernel_three.reshape(576, 128),
        bias_three.reshape(1, 128),
        kernel_four.reshape(1, 128),
        bias_four,
    )


def solution(mesh):
    placed = (
        P("pb", "slab", None, None),
        P(None, "pb", None, None),
        P(), P("pb"), P(), P(), P(), P(), P(), P(), P(), P(), P(),
    )
    return jax.shard_map(
        per_device, mesh=mesh, in_specs=placed, out_specs=P("pb", None), check_vma=False
    )
```
